128 devices in a mesh: face: 8 (over y, z_hi), tile: 16 (over x, z_lo, core).
Axes of the slice: x: 4, y: 4, z: 4 (z_hi: 2, z_lo: 2; z = z_hi * 2 + z_lo), core: 2. Of those that a mesh axis runs over, the one named last changes fastest.
Arguments:
- latitude_rows: bfloat16 [512, 4096, 128], P(None, ('face', 'tile')), may hold values from -6 to 6
- tile_order: int32 [512], replicated, may hold values from 0 to 511, each once
- neighbours: int32 [512, 8], P(('face', 'tile')), may hold values from 0 to 511, as said below
- rotations: int32 [512, 8], P(('face', 'tile')), may hold values from 0 to 3
- w_first: bfloat16 [3, 3, 128, 128], replicated, may hold values from -0.1875 to 0.1875
- b_first: float32 [128], replicated, may hold values from -3 to 3
- w_second: bfloat16 [3, 3, 128, 128], replicated, may hold values from -0.1875 to 0.1875
- b_second: float32 [128], replicated, may hold values from -3 to 3
Outputs:
- level_output: bfloat16 [512, 64, 64, 128], P(('face', 'tile'))
The draws below stay inside these ranges and needn't reach their ends.
Inputs may be any that keep to these rules, and one draw needn't show every extreme that they name: `neighbours`: tiles are held in order, 4 a device, devices ordered face-major. Entry k of a row names a tile held by the device whose face index and tile index differ, counted cyclically, from those of the device that holds the row's tile by (-1,0), (+1,0), (0,-1), (0,+1), (-1,-1), (-1,+1), (+1,-1), (+1,+1) for k = 0 to 7.
All inputs are finite; a program needn't handle non-finite values.
Results may differ from the reference program's by a relative error of at most 0.0033.
Values may be sent and summed in bfloat16 or wider, within the bound.
A program may use at most 64 MiB of HBM per device.

```python
from functools import partial
import jax
import jax.numpy as jnp
from jax import lax

SIDE = 64
CHANNELS = 128
TILES_DEV = 4
FACE_RANKS = 8
TILE_RANKS = 16
TILES = 512


def draw_neighbours(key, part):
    total = TILES_DEV * FACE_RANKS * TILE_RANKS
    tile_ids = jnp.arange(total, dtype=jnp.int32)
    home = tile_ids // TILES_DEV
    home_face = home // TILE_RANKS
    home_tile = home % TILE_RANKS
    local_key = jax.random.fold_in(key, 37)
    local_slot = jax.random.randint(local_key, (total, 8), 0, TILES_DEV, dtype=jnp.int32)
    face_step = jnp.array([-1, 1, 0, 0, -1, -1, 1, 1], jnp.int32)[None]
    tile_step = jnp.array([0, 0, -1, 1, -1, 1, -1, 1], jnp.int32)[None]
    owner_face = (home_face[:, None] + face_step) % FACE_RANKS
    owner_tile = (home_tile[:, None] + tile_step) % TILE_RANKS
    owner = owner_face * TILE_RANKS + owner_tile
    return (owner * TILES_DEV + local_slot).astype(jnp.int32)


def touch_ends(result, own_key, smallest, high):
    extent = result.shape
    place = [jax.random.randint(jax.random.fold_in(own_key, axis), (), 0, extent[axis]) for axis in range(len(extent))]
    result = result.at[tuple(place)].set(smallest)
    longest = extent.index(max(extent))
    place[longest] = (place[longest] + 1) % extent[longest]
    return result.at[tuple(place)].set(high)


def block_scale(key, extent, pieces, low, largest):
    level = 1.0
    for axis_at, blocks in pieces:
        heights = jax.random.uniform(jax.random.fold_in(jax.random.fold_in(key, 6), axis_at), (blocks,), jnp.float32, low / len(pieces), largest / len(pieces))
        level = level * jnp.repeat(jnp.exp(heights), extent[axis_at] // blocks).reshape((-1,) + (1,) * (len(extent) - 1 - axis_at))
    return level


def normal_values(own_key, shape, scale, limit, shards=(), kind=jnp.bfloat16):
    entries = jax.random.normal(own_key, shape, jnp.float32) * scale
    if len(shards) > 0:
        entries = block_scale(own_key, shape, shards, -0.22, 0.18) * entries
    return jnp.clip(entries, min=-limit, max=limit).astype(kind)


def setup_inputs(seed: int = 0) -> dict:
    splits = jax.random.split(jax.random.key(seed), 9)
    latitude_rows = normal_values(splits[0], (TILES, SIDE * SIDE, CHANNELS), 1.0, 6.0, ((1, 128),))
    tile_order = jax.random.permutation(splits[1], TILES).astype(jnp.int32)
    neighbours = draw_neighbours(jax.random.fold_in(splits[8], 71), 0)
    rotations = touch_ends(jax.random.randint(splits[3], (TILES, 8), 0, 4), jax.random.fold_in(splits[3], 1), 0, 3).astype(jnp.int32)
    w_first = normal_values(splits[4], (3, 3, CHANNELS, CHANNELS), (9 * CHANNELS) ** -0.5, 0.1875)
    b_first = normal_values(splits[5], (CHANNELS,), 0.5, 3.0, (), jnp.float32)
    w_second = normal_values(splits[6], (3, 3, CHANNELS, CHANNELS), (9 * CHANNELS) ** -0.5, 0.1875)
    b_second = normal_values(splits[7], (CHANNELS,), 0.5, 3.0, (), jnp.float32)
    return {"latitude_rows": latitude_rows, "tile_order": tile_order, "neighbours": neighbours, "rotations": rotations, "w_first": w_first, "b_first": b_first, "w_second": w_second, "b_second": b_second}


def convolve(padded, weight, bias):
    summed = lax.conv_general_dilated(padded, weight, (1, 1), "VALID", dimension_numbers=("NHWC", "HWIO", "NHWC"), preferred_element_type=jnp.float32)
    return summed + bias


def pad_one(source_tiles, centre, sources, turns):
    turners = [partial(jnp.rot90, k=quarter, axes=(0, 1)) for quarter in range(4)]

    def rotate_tile(other, rotation):
        return lax.switch(rotation, turners, other)

    others = jnp.take(source_tiles, sources, axis=0)
    turned = jax.vmap(rotate_tile)(others, turns)
    upper = jnp.concatenate([turned[4, -1, -1][None], turned[0, -1], turned[5, -1, 0][None]], 0)
    lower = jnp.concatenate([turned[6, 0, -1][None], turned[1, 0], turned[7, 0, 0][None]], 0)
    middle = jnp.concatenate([turned[2][:, -1][:, None], centre, turned[3][:, 0][:, None]], 1)
    return jnp.concatenate([upper[None], middle, lower[None]], 0)


def reference(latitude_rows, tile_order, neighbours, rotations, w_first, b_first, w_second, b_second):
    nested = jnp.take(latitude_rows, tile_order, axis=0).reshape(TILES, SIDE, SIDE, CHANNELS)

    def first_layer(inputs):
        centre, sources, turns = inputs
        padded = pad_one(nested, centre, sources, turns)
        first = convolve(padded[None], w_first, b_first)[0]
        return jax.nn.gelu(first, approximate=False).astype(jnp.bfloat16)

    hidden = lax.map(first_layer, (nested, neighbours, rotations))

    def second_layer(inputs):
        centre, sources, turns, residual_tile = inputs
        padded = pad_one(hidden, centre, sources, turns)
        second = convolve(padded[None], w_second, b_second)[0]
        return (residual_tile.astype(jnp.float32) + second).astype(jnp.bfloat16)

    return lax.map(second_layer, (hidden, neighbours, rotations, nested))
```

```python
import jax
import jax.numpy as jnp
import numpy as np
from jax import lax
from jax.experimental import pallas as pl
from jax.experimental.pallas import tpu as pltpu
from jax.sharding import PartitionSpec as P

SIDE = 64
CH = 128
TILES = 4
RANKS = 128
BLOCK = 32
WIDE = 80
LEFT = 8
PAIRS = 8
MESH = pl.DeviceIdType.MESH
BF16, F32 = jnp.bfloat16, jnp.float32

STRIP_TABLE = np.array(
    [
        [1, 2, 0, 3],
        [0, 3, 1, 2],
        [3, 1, 2, 0],
        [2, 0, 3, 1],
        [1, 2, 0, 3],
        [1, 2, 0, 3],
        [0, 3, 1, 2],
        [0, 3, 1, 2],
    ],
    np.int32,
)
FLIP_TABLE = np.array(
    [
        [0, 0, 1, 1],
        [0, 0, 1, 1],
        [0, 1, 1, 0],
        [0, 1, 1, 0],
        [0, 0, 1, 1],
        [0, 0, 1, 1],
        [0, 0, 1, 1],
        [0, 0, 1, 1],
    ],
    np.int32,
)
STEPS = ((-1, 0), (1, 0), (0, -1), (0, 1), (-1, -1), (-1, 1), (1, -1), (1, 1))


def displaced(i):
    f, t = lax.axis_index("face"), lax.axis_index("tile")
    x, c = t // 4, t % 2
    z, y = (f % 2) * 2 + (t // 2) % 2, f // 2
    x = (x + i % 4) % 4
    y = (y + (i // 4) % 4) % 4
    z = (z + (i // 16) % 4) % 4
    c = (c + i // 64) % 2
    return y * 2 + z // 2, x * 4 + (z % 2) * 2 + c


def gelu(v):
    return 0.5 * v * (1.0 + lax.erf(v * np.float32(0.5**0.5)))


def kernel(
    order, table, lat, near, turns, w1, b1, w2, b2, out,
    sent, nested, pad1, pad2, cols, wide1, wide2, lhs, border, edge,
    ask, asked, asked_s, pool, give, get, give_c, get_c,
    send_sem, recv_sem, ask_send, ask_recv, ask_copy, halo_send, halo_recv, corner_send, corner_recv,
):
    face, tile = lax.axis_index("face"), lax.axis_index("tile")
    me = face * 16 + tile

    def beside(k, sign):
        df, dt = STEPS[k]
        return (face + 8 + sign * df) % 8, (tile + 16 + sign * dt) % 16

    def gather(j):
        def step(d8, _):
            for u in range(8):
                d = d8 * 8 + u
                sent[j, d] = lat[order[d * TILES + j]]
            return 0

        lax.fori_loop(0, RANKS // 8, step, 0)
        nested[j, me] = lat[order[me * TILES + j]]

    def send(j):
        def step(i, _):
            f, t = displaced((i * 37) % RANKS)
            pltpu.make_async_remote_copy(
                src_ref=sent.at[j, f * 16 + t],
                dst_ref=nested.at[j, me],
                send_sem=send_sem.at[j],
                recv_sem=recv_sem.at[j],
                device_id=(f, t),
                device_id_type=MESH,
            ).start()
            return 0

        lax.fori_loop(1, RANKS, step, 0)

    def all_of(j):
        view = nested.at[j, pl.ds(0, RANKS - 1)]
        return pltpu.make_async_remote_copy(
            src_ref=view,
            dst_ref=view,
            send_sem=send_sem.at[j],
            recv_sem=recv_sem.at[j],
            device_id=(face, tile),
            device_id_type=MESH,
        )

    ask[...] = jnp.zeros_like(ask)
    ask[0:4, 0:8] = near[...]
    ask[4:8, 0:8] = turns[...]
    gather(0)
    gather(1)
    send(0)
    gather(2)
    send(1)
    gather(3)
    send(2)
    send(3)

    asks = [
        pltpu.make_async_remote_copy(
            src_ref=ask,
            dst_ref=asked.at[k],
            send_sem=ask_send.at[k],
            recv_sem=ask_recv.at[k],
            device_id=beside(k, 1),
            device_id_type=MESH,
        )
        for k in range(8)
    ]
    for a in asks:
        a.start()

    for w, wide in ((w1, wide1), (w2, wide2)):
        zero = jnp.zeros((CH, CH), BF16)
        for q in range(4):
            for dx in range(3):
                at = pl.ds((q * 3 + dx) * CH, CH)
                wide[at, 0:CH] = w[q, dx] if q < 3 else zero
                wide[at, CH : 2 * CH] = w[q - 1, dx] if q > 0 else zero

    for a in asks:
        a.wait()
    fetch = pltpu.make_async_copy(asked, asked_s, ask_copy)
    fetch.start()
    fetch.wait()

    def halo_copies(level):
        copies = []
        for k in range(8):
            copies.append(
                pltpu.make_async_remote_copy(
                    src_ref=give.at[level, k] if k < 4 else give_c.at[level, k - 4],
                    dst_ref=get.at[level, k] if k < 4 else get_c.at[level, k - 4],
                    send_sem=halo_send.at[level, k],
                    recv_sem=halo_recv.at[level, k],
                    device_id=beside(k, -1),
                    device_id_type=MESH,
                )
            )
        return copies

    def pick(level, strips):
        for s in range(16):
            pool[level, s] = strips[s]
        r = lax.broadcasted_iota(jnp.int32, (SIDE, SIDE), 0)
        c = lax.broadcasted_iota(jnp.int32, (SIDE, SIDE), 1)
        mirror = jnp.where(r + c == SIDE - 1, 1.0, 0.0).astype(BF16)
        turned = jnp.dot(mirror, jnp.concatenate(strips, axis=1), preferred_element_type=F32).astype(BF16)
        for s in range(16):
            pool[level, 16 + s] = turned[:, s * CH : (s + 1) * CH]
        for k in range(8):
            for j in range(TILES):
                source = table[k * 4 + asked_s[k, 4 + j, k]] + (asked_s[k, j, k] % TILES) * 4
                if k < 4:
                    give[level, k, j] = pool[level, source]
                elif k % 2 == 0:
                    give_c[level, k - 4, j] = pool[level, source, SIDE - 16 :, :]
                else:
                    give_c[level, k - 4, j] = pool[level, source, 0:16, :]

    def place(level, pad):
        for j in range(TILES):
            flat = pad.at[j].reshape(66 * WIDE, CH)
            pad[j, 0, LEFT : LEFT + SIDE, :] = get[level, 0, j].astype(F32)
            pad[j, 65, LEFT : LEFT + SIDE, :] = get[level, 1, j].astype(F32)
            flat[pl.ds(WIDE + LEFT - 1, SIDE, stride=WIDE), :] = get[level, 2, j].astype(F32)
            flat[pl.ds(WIDE + LEFT + SIDE, SIDE, stride=WIDE), :] = get[level, 3, j].astype(F32)
            for k in range(4):
                block = get_c[level, k, j].astype(F32)
                row = block[15:16] if k % 2 == 0 else block[0:1]
                at_r = 0 if k < 2 else 65
                at_c = LEFT - 1 if k % 2 == 0 else LEFT + SIDE
                pad[j, at_r, at_c : at_c + 1, :] = row

    def columns(j, pad, with_centre):
        def step(r, _):
            if with_centre is not None:
                centre = with_centre(r)
                pad[j, r + 1, LEFT : LEFT + SIDE, :] = centre.astype(F32)
            for dx in range(3):
                cols[dx, (r + 1) // 2, (r + 1) % 2] = pad[j, r + 1, LEFT - 1 + dx : LEFT - 1 + dx + SIDE, :].astype(BF16)
            return 0

        lax.fori_loop(0, SIDE, step, 0)

    def convolve(wide, done):
        def step(b, _):
            p = b * PAIRS
            pieces = []
            for q in range(4):
                for dx in range(3):
                    pieces.append(cols[dx, pl.ds(p + q // 2, PAIRS), q % 2].reshape(PAIRS * SIDE, CH))
            acc = jnp.dot(jnp.concatenate(pieces, axis=1), wide[...], preferred_element_type=F32)
            done(b, acc)
            return 0

        lax.fori_loop(0, SIDE // (2 * PAIRS), step, 0)

    def ring(j, pad, weight, rows):
        flat = pad.at[j].reshape(66 * WIDE, CH)
        n = 4 * rows
        for q in range(3):
            for dx in range(3):
                to = pl.ds((q * 3 + dx) * CH, CH)
                for s in range(n):
                    side, depth = s % 4, s // 4
                    line = depth if side % 2 == 0 else SIDE - 1 - depth
                    if side < 2:
                        v = pad[j, line + q, LEFT - 1 + dx : LEFT - 1 + dx + SIDE, :]
                    else:
                        v = flat[pl.ds(q * WIDE + LEFT - 1 + line + dx, SIDE, stride=WIDE), :]
                    border[s * SIDE : (s + 1) * SIDE, to] = v.astype(BF16)
        return jnp.dot(border[0 : n * SIDE, :], weight, preferred_element_type=F32)

    bias1, bias2 = b1[...], b2[...]
    both1 = jnp.concatenate([bias1, bias1], axis=1)
    both2 = jnp.concatenate([bias2, bias2], axis=1)

    def whole_tile(j, _):
        all_of(j).wait_recv()

        def centre(r):
            return nested[j, pl.ds(2 * r, 2)].reshape(SIDE, CH)

        columns(j, pad1, centre)

        @pl.when(j == TILES - 1)
        def _():
            strips = []
            for i in range(TILES):
                flat = pad1.at[i].reshape(66 * WIDE, CH)
                strips.append(nested[i, 0:2].reshape(SIDE, CH))
                strips.append(nested[i, RANKS - 2 : RANKS].reshape(SIDE, CH))
                strips.append(flat[pl.ds(WIDE + LEFT, SIDE, stride=WIDE), :].astype(BF16))
                strips.append(flat[pl.ds(WIDE + LEFT + SIDE - 1, SIDE, stride=WIDE), :].astype(BF16))
            pick(0, strips)
            for h in halo_copies(0):
                h.start()

        def first_done(b, acc):
            hid = gelu(acc + both1).reshape(PAIRS, SIDE, 2 * CH)
            for p in range(PAIRS):
                row = 2 * (b * PAIRS + p) + 1
                pad2[j, row, LEFT : LEFT + SIDE, :] = hid[p, :, :CH]
                pad2[j, row + 1, LEFT : LEFT + SIDE, :] = hid[p, :, CH:]

        convolve(wide1, first_done)

        @pl.when(j == TILES - 1)
        def _():
            for h in halo_copies(0):
                h.wait_recv()
            place(0, pad1)
            weight = w1[...].reshape(9 * CH, CH)

            def one(i, _):
                hid = gelu(ring(i, pad1, weight, 1) + bias1)
                flat = pad2.at[i].reshape(66 * WIDE, CH)
                pad2[i, 1, LEFT : LEFT + SIDE, :] = hid[0:64]
                pad2[i, SIDE, LEFT : LEFT + SIDE, :] = hid[64:128]
                flat[pl.ds(WIDE + LEFT, SIDE, stride=WIDE), :] = hid[128:192]
                flat[pl.ds(WIDE + LEFT + SIDE - 1, SIDE, stride=WIDE), :] = hid[192:256]
                for s in range(4):
                    edge[i * 4 + s] = hid[s * 64 : (s + 1) * 64].astype(BF16)
                return 0

            lax.fori_loop(0, TILES, one, 0)
            pick(1, [edge[s] for s in range(16)])
            for h in halo_copies(1):
                h.start()

        columns(j, pad2, None)

        def second_done(b, acc):
            acc = (acc + both2).reshape(PAIRS, SIDE, 2 * CH)
            for p in range(PAIRS):
                for half in range(2):
                    row = 2 * (b * PAIRS + p) + half
                    v = acc[p, :, half * CH : (half + 1) * CH] + pad1[j, row + 1, LEFT : LEFT + SIDE, :]
                    out[j, row] = v.astype(BF16)
                    lhs[j, 0, row] = v[0:16]
                    lhs[j, 1, row] = v[SIDE - 16 :]

        convolve(wide2, second_done)
        return 0

    lax.fori_loop(0, TILES, whole_tile, 0)

    for h in halo_copies(1):
        h.wait_recv()
    place(1, pad2)
    weight = w2[...].reshape(9 * CH, CH)

    def last(i, _):
        acc = ring(i, pad2, weight, 2) + bias2
        flat = pad1.at[i].reshape(66 * WIDE, CH)
        for s in range(4, 8):
            pass
        for s in (4, 5, 6, 7, 0, 1, 2, 3):
            side, depth = s % 4, s // 4
            line = depth if side % 2 == 0 else SIDE - 1 - depth
            v = acc[s * SIDE : (s + 1) * SIDE]
            if side < 2:
                v = v + pad1[i, line + 1, LEFT : LEFT + SIDE, :]
                lhs[i, 0, line] = v[0:16]
                lhs[i, 1, line] = v[SIDE - 16 :]
                out[i, line] = v.astype(BF16)
            else:
                v = v + flat[pl.ds(WIDE + LEFT + line, SIDE, stride=WIDE), :]
                block = lhs.at[i, side - 2].reshape(SIDE * 16, CH)
                block[pl.ds(line % 16, SIDE, stride=16), :] = v
        out[i, :, 0:16, :] = lhs[i, 0].astype(BF16)
        out[i, :, SIDE - 16 :, :] = lhs[i, 1].astype(BF16)
        return 0

    lax.fori_loop(0, TILES, last, 0)

    for j in range(TILES):
        all_of(j).wait_send()
    for level in range(2):
        for h in halo_copies(level):
            h.wait_send()


def shards(latitude_rows, tile_order, neighbours, rotations, w_first, b_first, w_second, b_second):
    vmem = pl.BlockSpec(memory_space=pltpu.VMEM)
    smem = pl.BlockSpec(memory_space=pltpu.SMEM)
    table = jnp.asarray((FLIP_TABLE * 16 + STRIP_TABLE).reshape(-1))
    dma = pltpu.SemaphoreType.DMA
    return pl.pallas_call(
        kernel,
        out_shape=jax.ShapeDtypeStruct((TILES, SIDE, SIDE, CH), BF16),
        in_specs=[smem, smem] + [vmem] * 7,
        out_specs=vmem,
        scratch_shapes=[
            pltpu.VMEM((TILES, RANKS, BLOCK, CH), BF16),
            pltpu.VMEM((TILES, RANKS, BLOCK, CH), BF16),
            pltpu.VMEM((TILES, SIDE + 2, WIDE, CH), F32),
            pltpu.VMEM((TILES, SIDE + 2, WIDE, CH), F32),
            pltpu.VMEM((3, SIDE // 2 + 1, 2, SIDE, CH), BF16),
            pltpu.VMEM((12 * CH, 2 * CH), BF16),
            pltpu.VMEM((12 * CH, 2 * CH), BF16),
            pltpu.VMEM((TILES, 2, SIDE, 16, CH), F32),
            pltpu.VMEM((8 * SIDE, 9 * CH), BF16),
            pltpu.VMEM((16, SIDE, CH), BF16),
            pltpu.VMEM((8, CH), jnp.int32),
            pltpu.VMEM((8, 8, CH), jnp.int32),
            pltpu.SMEM((8, 8, CH), jnp.int32),
            pltpu.VMEM((2, 32, SIDE, CH), BF16),
            pltpu.VMEM((2, 4, TILES, SIDE, CH), BF16),
            pltpu.VMEM((2, 4, TILES, SIDE, CH), BF16),
            pltpu.VMEM((2, 4, TILES, 16, CH), BF16),
            pltpu.VMEM((2, 4, TILES, 16, CH), BF16),
            dma((TILES,)),
            dma((TILES,)),
            dma((8,)),
            dma((8,)),
            dma,
            dma((2, 8)),
            dma((2, 8)),
            dma((2, 8)),
            dma((2, 8)),
        ],
        compiler_params=pltpu.CompilerParams(has_side_effects=True, vmem_limit_bytes=62 << 20),
        name="level",
    )(
        tile_order, table, latitude_rows, neighbours, rotations,
        w_first, b_first.reshape(1, CH), w_second, b_second.reshape(1, CH),
    )


def solution(mesh):
    return jax.shard_map(
        shards,
        mesh=mesh,
        in_specs=(
            P(None, ("face", "tile"), None),
            P(),
            P(("face", "tile"), None),
            P(("face", "tile"), None),
            P(),
            P(),
            P(),
            P(),
        ),
        out_specs=P(("face", "tile"), None, None, None),
        check_vma=False,
    )
```

```python
import jax
import jax.numpy as jnp
import numpy as np
from jax import lax
from jax.experimental import pallas as pl
from jax.experimental.pallas import tpu as pltpu
from jax.sharding import PartitionSpec as P

SIDE = 64
CH = 128
TILES = 4
RANKS = 128
BLOCK = 32
WIDE = 80
LEFT = 8
PAIRS = 8
MESH = pl.DeviceIdType.MESH
BF16, F32 = jnp.bfloat16, jnp.float32

STRIP_TABLE = np.array(
    [
        [1, 2, 0, 3],
        [0, 3, 1, 2],
        [3, 1, 2, 0],
        [2, 0, 3, 1],
        [1, 2, 0, 3],
        [1, 2, 0, 3],
        [0, 3, 1, 2],
        [0, 3, 1, 2],
    ],
    np.int32,
)
FLIP_TABLE = np.array(
    [
        [0, 0, 1, 1],
        [0, 0, 1, 1],
        [0, 1, 1, 0],
        [0, 1, 1, 0],
        [0, 0, 1, 1],
        [0, 0, 1, 1],
        [0, 0, 1, 1],
        [0, 0, 1, 1],
    ],
    np.int32,
)
STEPS = ((-1, 0), (1, 0), (0, -1), (0, 1), (-1, -1), (-1, 1), (1, -1), (1, 1))


def displaced(i):
    f, t = lax.axis_index("face"), lax.axis_index("tile")
    x, c = t // 4, t % 2
    z, y = (f % 2) * 2 + (t // 2) % 2, f // 2
    x = (x + i % 4) % 4
    y = (y + (i // 4) % 4) % 4
    z = (z + (i // 16) % 4) % 4
    c = (c + i // 64) % 2
    return y * 2 + z // 2, x * 4 + (z % 2) * 2 + c


def gelu(v):
    return 0.5 * v * (1.0 + lax.erf(v * np.float32(0.5**0.5)))


def kernel(
    order_h, table_h, lat_h, near_h, turns_h, w1_h, b1_h, w2_h, b2_h, out,
    order, table, lat, near, turns, w1, b1, w2, b2, load_sem,
    sent, nested, pad1, pad2, cols, wide1, wide2, lhs, border, edge,
    ask, asked, asked_s, pool, give, get, give_c, get_c,
    send_sem, recv_sem, ask_send, ask_recv, ask_copy, halo_send, halo_recv, corner_send, corner_recv,
):
    face, tile = lax.axis_index("face"), lax.axis_index("tile")
    me = face * 16 + tile

    def beside(k, sign):
        df, dt = STEPS[k]
        return (face + 8 + sign * df) % 8, (tile + 16 + sign * dt) % 16

    def gather(j):
        def step(d8, _):
            for u in range(8):
                d = d8 * 8 + u
                sent[j, d] = lat[order[d * TILES + j]]
            return 0

        lax.fori_loop(0, RANKS // 8, step, 0)
        nested[j, me] = lat[order[me * TILES + j]]

    def send(j):
        def step(i, _):
            f, t = displaced((i * 37) % RANKS)
            pltpu.make_async_remote_copy(
                src_ref=sent.at[j, f * 16 + t],
                dst_ref=nested.at[j, me],
                send_sem=send_sem.at[j],
                recv_sem=recv_sem.at[j],
                device_id=(f, t),
                device_id_type=MESH,
            ).start()
            return 0

        lax.fori_loop(1, RANKS, step, 0)

    def all_of(j):
        view = nested.at[j, pl.ds(0, RANKS - 1)]
        return pltpu.make_async_remote_copy(
            src_ref=view,
            dst_ref=view,
            send_sem=send_sem.at[j],
            recv_sem=recv_sem.at[j],
            device_id=(face, tile),
            device_id_type=MESH,
        )

    loads = [
        pltpu.make_async_copy(src, dst, load_sem.at[i])
        for i, (src, dst) in enumerate((
            (order_h, order), (near_h, near), (turns_h, turns), (lat_h, lat), (table_h, table),
            (w1_h, w1), (b1_h, b1), (w2_h, w2), (b2_h, b2),
        ))
    ]
    for load in loads:
        load.start()
    for load in loads[:4]:
        load.wait()
    ask[...] = jnp.zeros_like(ask)
    ask[0:4, 0:8] = near[...]
    ask[4:8, 0:8] = turns[...]
    gather(0)
    gather(1)
    asks = [
        pltpu.make_async_remote_copy(
            src_ref=ask,
            dst_ref=asked.at[k],
            send_sem=ask_send.at[k],
            recv_sem=ask_recv.at[k],
            device_id=beside(k, 1),
            device_id_type=MESH,
        )
        for k in range(8)
    ]
    for a in asks:
        a.start()

    send(0)
    gather(2)
    send(1)
    gather(3)
    send(2)
    send(3)

    for load in loads[4:]:
        load.wait()

    for dx in range(3):
        cols[dx, 0, 0] = jnp.zeros((SIDE, CH), BF16)
        cols[dx, SIDE // 2, 1] = jnp.zeros((SIDE, CH), BF16)

    for w, wide in ((w1, wide1), (w2, wide2)):
        zero = jnp.zeros((CH, CH), BF16)
        for q in range(4):
            for dx in range(3):
                at = pl.ds((q * 3 + dx) * CH, CH)
                wide[at, 0:CH] = w[q, dx] if q < 3 else zero
                wide[at, CH : 2 * CH] = w[q - 1, dx] if q > 0 else zero

    def halo_copies(level):
        copies = []
        for k in range(8):
            copies.append(
                pltpu.make_async_remote_copy(
                    src_ref=give.at[level, k] if k < 4 else give_c.at[level, k - 4],
                    dst_ref=get.at[level, k] if k < 4 else get_c.at[level, k - 4],
                    send_sem=halo_send.at[level, k],
                    recv_sem=halo_recv.at[level, k],
                    device_id=beside(k, -1),
                    device_id_type=MESH,
                )
            )
        return copies

    def pick(level, strips):
        for s in range(16):
            pool[level, s] = strips[s]
        r = lax.broadcasted_iota(jnp.int32, (SIDE, SIDE), 0)
        c = lax.broadcasted_iota(jnp.int32, (SIDE, SIDE), 1)
        mirror = jnp.where(r + c == SIDE - 1, 1.0, 0.0).astype(BF16)
        turned = jnp.dot(mirror, jnp.concatenate(strips, axis=1), preferred_element_type=F32).astype(BF16)
        for s in range(16):
            pool[level, 16 + s] = turned[:, s * CH : (s + 1) * CH]
        for k in range(8):
            for j in range(TILES):
                source = table[k * 4 + asked_s[k, 4 + j, k]] + (asked_s[k, j, k] % TILES) * 4
                if k < 4:
                    give[level, k, j] = pool[level, source]
                elif k % 2 == 0:
                    give_c[level, k - 4, j] = pool[level, source, SIDE - 16 :, :]
                else:
                    give_c[level, k - 4, j] = pool[level, source, 0:16, :]

    def place(level, pad):
        for j in range(TILES):
            flat = pad.at[j].reshape(66 * WIDE, CH)
            pad[j, 0, LEFT : LEFT + SIDE, :] = get[level, 0, j].astype(F32)
            pad[j, 65, LEFT : LEFT + SIDE, :] = get[level, 1, j].astype(F32)
            flat[pl.ds(WIDE + LEFT - 1, SIDE, stride=WIDE), :] = get[level, 2, j].astype(F32)
            flat[pl.ds(WIDE + LEFT + SIDE, SIDE, stride=WIDE), :] = get[level, 3, j].astype(F32)
            for k in range(4):
                block = get_c[level, k, j].astype(F32)
                row = block[15:16] if k % 2 == 0 else block[0:1]
                at_r = 0 if k < 2 else 65
                at_c = LEFT - 1 if k % 2 == 0 else LEFT + SIDE
                pad[j, at_r, at_c : at_c + 1, :] = row

    def columns(j, pad, with_centre):
        def step(r, _):
            if with_centre is not None:
                centre = with_centre(r)
                pad[j, r + 1, LEFT : LEFT + SIDE, :] = centre.astype(F32)
            for dx in range(3):
                cols[dx, (r + 1) // 2, (r + 1) % 2] = pad[j, r + 1, LEFT - 1 + dx : LEFT - 1 + dx + SIDE, :].astype(BF16)
            return 0

        lax.fori_loop(0, SIDE, step, 0)

    def convolve(wide, done):
        def step(b, _):
            p = b * PAIRS
            pieces = []
            for q in range(4):
                for dx in range(3):
                    pieces.append(cols[dx, pl.ds(p + q // 2, PAIRS), q % 2].reshape(PAIRS * SIDE, CH))
            acc = jnp.dot(jnp.concatenate(pieces, axis=1), wide[...], preferred_element_type=F32)
            done(b, acc)
            return 0

        lax.fori_loop(0, SIDE // (2 * PAIRS), step, 0)

    def ring(j, pad, weight, depth):
        flat = pad.at[j].reshape(66 * WIDE, CH)
        for q in range(3):
            for dx in range(3):
                to = pl.ds((q * 3 + dx) * CH, CH)
                for s in range(4):
                    line = depth if s % 2 == 0 else SIDE - 1 - depth
                    if s < 2:
                        v = pad[j, line + q, LEFT - 1 + dx : LEFT - 1 + dx + SIDE, :]
                    else:
                        v = flat[pl.ds(q * WIDE + LEFT - 1 + line + dx, SIDE, stride=WIDE), :]
                    border[s * SIDE : (s + 1) * SIDE, to] = v.astype(BF16)
        return jnp.dot(border[...], weight, preferred_element_type=F32)

    bias1, bias2 = b1[...], b2[...]
    both1 = jnp.concatenate([bias1, bias1], axis=1)
    both2 = jnp.concatenate([bias2, bias2], axis=1)

    def whole_tile(j, _):
        all_of(j).wait_recv()

        def centre(r):
            return nested[j, pl.ds(2 * r, 2)].reshape(SIDE, CH)

        columns(j, pad1, centre)

        @pl.when(j == TILES - 1)
        def _():
            strips = []
            for i in range(TILES):
                flat = pad1.at[i].reshape(66 * WIDE, CH)
                strips.append(nested[i, 0:2].reshape(SIDE, CH))
                strips.append(nested[i, RANKS - 2 : RANKS].reshape(SIDE, CH))
                strips.append(flat[pl.ds(WIDE + LEFT, SIDE, stride=WIDE), :].astype(BF16))
                strips.append(flat[pl.ds(WIDE + LEFT + SIDE - 1, SIDE, stride=WIDE), :].astype(BF16))
            pick(0, strips)
            for h in halo_copies(0):
                h.start()

        def first_done(b, acc):
            hid = gelu(acc + both1).reshape(PAIRS, SIDE, 2 * CH)
            for p in range(PAIRS):
                row = 2 * (b * PAIRS + p) + 1
                pad2[j, row, LEFT : LEFT + SIDE, :] = hid[p, :, :CH]
                pad2[j, row + 1, LEFT : LEFT + SIDE, :] = hid[p, :, CH:]

        convolve(wide1, first_done)

        @pl.when(j == TILES - 1)
        def _():
            for h in halo_copies(0):
                h.wait_recv()
            place(0, pad1)
            weight = w1[...].reshape(9 * CH, CH)

            def one(i, _):
                hid = gelu(ring(i, pad1, weight, 0) + bias1)
                flat = pad2.at[i].reshape(66 * WIDE, CH)
                pad2[i, 1, LEFT : LEFT + SIDE, :] = hid[0:64]
                pad2[i, SIDE, LEFT : LEFT + SIDE, :] = hid[64:128]
                flat[pl.ds(WIDE + LEFT, SIDE, stride=WIDE), :] = hid[128:192]
                flat[pl.ds(WIDE + LEFT + SIDE - 1, SIDE, stride=WIDE), :] = hid[192:256]
                for s in range(4):
                    edge[i * 4 + s] = hid[s * 64 : (s + 1) * 64].astype(BF16)
                return 0

            lax.fori_loop(0, TILES, one, 0)
            pick(1, [edge[s] for s in range(16)])
            for h in halo_copies(1):
                h.start()

        columns(j, pad2, None)

        def second_done(b, acc):
            acc = (acc + both2).reshape(PAIRS, SIDE, 2 * CH)
            for p in range(PAIRS):
                for half in range(2):
                    row = 2 * (b * PAIRS + p) + half
                    v = acc[p, :, half * CH : (half + 1) * CH] + pad1[j, row + 1, LEFT : LEFT + SIDE, :]
                    out[j, row] = v.astype(BF16)
                    lhs[j, 0, row] = v[0:16]
                    lhs[j, 1, row] = v[SIDE - 16 :]

        convolve(wide2, second_done)
        return 0

    for a in asks:
        a.wait()
    fetch = pltpu.make_async_copy(asked, asked_s, ask_copy)
    fetch.start()
    fetch.wait()

    lax.fori_loop(0, TILES, whole_tile, 0)

    weight = w2[...].reshape(9 * CH, CH)

    def mend(i, depth):
        acc = ring(i, pad2, weight, depth) + bias2
        flat = pad1.at[i].reshape(66 * WIDE, CH)
        for side in (2, 3, 0, 1):
            line = depth if side % 2 == 0 else SIDE - 1 - depth
            v = acc[side * SIDE : (side + 1) * SIDE]
            if side < 2:
                v = v + pad1[i, line + 1, LEFT : LEFT + SIDE, :]
                lhs[i, 0, line] = v[0:16]
                lhs[i, 1, line] = v[SIDE - 16 :]
                out[i, line] = v.astype(BF16)
            else:
                v = v + flat[pl.ds(WIDE + LEFT + line, SIDE, stride=WIDE), :]
                block = lhs.at[i, side - 2].reshape(SIDE * 16, CH)
                block[pl.ds(line % 16, SIDE, stride=16), :] = v

    def inner_ring(i, _):
        mend(i, 1)
        return 0

    def outer_ring(i, _):
        mend(i, 0)
        out[i, :, 0:16, :] = lhs[i, 0].astype(BF16)
        out[i, :, SIDE - 16 :, :] = lhs[i, 1].astype(BF16)
        return 0

    lax.fori_loop(0, TILES, inner_ring, 0)
    for h in halo_copies(1):
        h.wait_recv()
    place(1, pad2)
    lax.fori_loop(0, TILES, outer_ring, 0)

    for j in range(TILES):
        all_of(j).wait_send()
    for level in range(2):
        for h in halo_copies(level):
            h.wait_send()


def shards(latitude_rows, tile_order, neighbours, rotations, w_first, b_first, w_second, b_second):
    vmem = pl.BlockSpec(memory_space=pltpu.VMEM)
    table = jnp.asarray((FLIP_TABLE * 16 + STRIP_TABLE).reshape(-1))
    dma = pltpu.SemaphoreType.DMA
    return pl.pallas_call(
        kernel,
        out_shape=jax.ShapeDtypeStruct((TILES, SIDE, SIDE, CH), BF16),
        in_specs=[pl.BlockSpec(memory_space=pltpu.HBM)] * 9,
        out_specs=vmem,
        scratch_shapes=[
            pltpu.SMEM((RANKS * TILES,), jnp.int32),
            pltpu.SMEM((32,), jnp.int32),
            pltpu.VMEM((RANKS * TILES, BLOCK, CH), BF16),
            pltpu.VMEM((TILES, 8), jnp.int32),
            pltpu.VMEM((TILES, 8), jnp.int32),
            pltpu.VMEM((3, 3, CH, CH), BF16),
            pltpu.VMEM((1, CH), F32),
            pltpu.VMEM((3, 3, CH, CH), BF16),
            pltpu.VMEM((1, CH), F32),
            dma((9,)),
            pltpu.VMEM((TILES, RANKS, BLOCK, CH), BF16),
            pltpu.VMEM((TILES, RANKS, BLOCK, CH), BF16),
            pltpu.VMEM((TILES, SIDE + 2, WIDE, CH), F32),
            pltpu.VMEM((TILES, SIDE + 2, WIDE, CH), F32),
            pltpu.VMEM((3, SIDE // 2 + 1, 2, SIDE, CH), BF16),
            pltpu.VMEM((12 * CH, 2 * CH), BF16),
            pltpu.VMEM((12 * CH, 2 * CH), BF16),
            pltpu.VMEM((TILES, 2, SIDE, 16, CH), F32),
            pltpu.VMEM((4 * SIDE, 9 * CH), BF16),
            pltpu.VMEM((16, SIDE, CH), BF16),
            pltpu.VMEM((8, CH), jnp.int32),
            pltpu.VMEM((8, 8, CH), jnp.int32),
            pltpu.SMEM((8, 8, CH), jnp.int32),
            pltpu.VMEM((2, 32, SIDE, CH), BF16),
            pltpu.VMEM((2, 4, TILES, SIDE, CH), BF16),
            pltpu.VMEM((2, 4, TILES, SIDE, CH), BF16),
            pltpu.VMEM((2, 4, TILES, 16, CH), BF16),
            pltpu.VMEM((2, 4, TILES, 16, CH), BF16),
            dma((TILES,)),
            dma((TILES,)),
            dma((8,)),
            dma((8,)),
            dma,
            dma((2, 8)),
            dma((2, 8)),
            dma((2, 8)),
            dma((2, 8)),
        ],
        compiler_params=pltpu.CompilerParams(has_side_effects=True, vmem_limit_bytes=47 << 20),
        name="level",
    )(
        *(
            pltpu.with_memory_space_constraint(v, pltpu.HBM)
            for v in (
                tile_order, table, latitude_rows, neighbours, rotations,
                w_first, b_first.reshape(1, CH), w_second, b_second.reshape(1, CH),
            )
        )
    )


def solution(mesh):
    return jax.shard_map(
        shards,
        mesh=mesh,
        in_specs=(
            P(None, ("face", "tile"), None),
            P(),
            P(("face", "tile"), None),
            P(("face", "tile"), None),
            P(),
            P(),
            P(),
            P(),
        ),
        out_specs=P(("face", "tile"), None, None, None),
        check_vma=False,
    )
```

```python
import jax
import jax.numpy as jnp
import numpy as np
from jax import lax
from jax.experimental import pallas as pl
from jax.experimental.pallas import tpu as pltpu
from jax.sharding import PartitionSpec as P

SIDE = 64
CH = 128
TILES = 4
RANKS = 128
BLOCK = 32
WIDE = 80
LEFT = 8
PAIRS = 8
MESH = pl.DeviceIdType.MESH
BF16, F32 = jnp.bfloat16, jnp.float32

STRIP_TABLE = np.array(
    [
        [1, 2, 0, 3],
        [0, 3, 1, 2],
        [3, 1, 2, 0],
        [2, 0, 3, 1],
        [1, 2, 0, 3],
        [1, 2, 0, 3],
        [0, 3, 1, 2],
        [0, 3, 1, 2],
    ],
    np.int32,
)
FLIP_TABLE = np.array(
    [
        [0, 0, 1, 1],
        [0, 0, 1, 1],
        [0, 1, 1, 0],
        [0, 1, 1, 0],
        [0, 0, 1, 1],
        [0, 0, 1, 1],
        [0, 0, 1, 1],
        [0, 0, 1, 1],
    ],
    np.int32,
)
STEPS = ((-1, 0), (1, 0), (0, -1), (0, 1), (-1, -1), (-1, 1), (1, -1), (1, 1))


def displaced(i):
    f, t = lax.axis_index("face"), lax.axis_index("tile")
    x, c = t // 4, t % 2
    z, y = (f % 2) * 2 + (t // 2) % 2, f // 2
    x = (x + i % 4) % 4
    y = (y + (i // 4) % 4) % 4
    z = (z + (i // 16) % 4) % 4
    c = (c + i // 64) % 2
    return y * 2 + z // 2, x * 4 + (z % 2) * 2 + c


def gelu(v):
    return 0.5 * v * (1.0 + lax.erf(v * np.float32(0.5**0.5)))


def kernel(
    order_h, table_h, lat_h, near_h, turns_h, w1_h, b1_h, w2_h, b2_h, out,
    order, table, area, near, turns, w1, b1, w2, b2, load_sem,
    sent, nested, pad1, pad2, wide1, wide2, lhs, border,
    lines, beyond, part_row, part_col, flat_tmp,
    ask, asked, asked_s, pool, give, get, give_c, get_c,
    send_sem, recv_sem, ask_send, ask_recv, ask_copy, halo_send, halo_recv, corner_send, corner_recv,
):
    face, tile = lax.axis_index("face"), lax.axis_index("tile")
    me = face * 16 + tile
    lat = area.reshape(RANKS * TILES, BLOCK, CH)
    cols = area.reshape(RANKS, 2, SIDE, CH)
    pairs = SIDE // 2 + 1

    def beside(k, sign):
        df, dt = STEPS[k]
        return (face + 8 + sign * df) % 8, (tile + 16 + sign * dt) % 16

    def gather(j):
        def step(d8, _):
            for u in range(8):
                d = d8 * 8 + u
                sent[j, d] = lat[order[d * TILES + j]]
            return 0

        lax.fori_loop(0, RANKS // 8, step, 0)
        nested[j, me] = lat[order[me * TILES + j]]

    def send(j):
        def step(i, _):
            f, t = displaced((i * 37) % RANKS)
            pltpu.make_async_remote_copy(
                src_ref=sent.at[j, f * 16 + t],
                dst_ref=nested.at[j, me],
                send_sem=send_sem.at[j],
                recv_sem=recv_sem.at[j],
                device_id=(f, t),
                device_id_type=MESH,
            ).start()
            return 0

        lax.fori_loop(1, RANKS, step, 0)

    def all_of(j):
        view = nested.at[j, pl.ds(0, RANKS - 1)]
        return pltpu.make_async_remote_copy(
            src_ref=view,
            dst_ref=view,
            send_sem=send_sem.at[j],
            recv_sem=recv_sem.at[j],
            device_id=(face, tile),
            device_id_type=MESH,
        )

    loads = [
        pltpu.make_async_copy(src, dst, load_sem.at[i])
        for i, (src, dst) in enumerate((
            (order_h, order), (near_h, near), (turns_h, turns), (lat_h, lat), (table_h, table),
            (w1_h, w1), (b1_h, b1), (w2_h, w2), (b2_h, b2),
        ))
    ]
    for load in loads:
        load.start()
    for load in loads[:4]:
        load.wait()
    ask[...] = jnp.zeros_like(ask)
    ask[0:4, 0:8] = near[...]
    ask[4:8, 0:8] = turns[...]
    gather(0)
    gather(1)
    asks = [
        pltpu.make_async_remote_copy(
            src_ref=ask,
            dst_ref=asked.at[k],
            send_sem=ask_send.at[k],
            recv_sem=ask_recv.at[k],
            device_id=beside(k, 1),
            device_id_type=MESH,
        )
        for k in range(8)
    ]
    for a in asks:
        a.start()

    send(0)
    gather(2)
    send(1)
    gather(3)
    send(2)
    send(3)

    for load in loads[4:]:
        load.wait()

    for pad in (pad1, pad2):
        for j in range(TILES):
            flat = pad.at[j].reshape(66 * WIDE, CH)
            for at_c in (LEFT - 1, LEFT + SIDE):
                flat[pl.ds(WIDE + at_c, SIDE, stride=WIDE), :] = jnp.zeros((SIDE, CH), F32)
    for j in range(TILES):
        pad2[j, 0] = jnp.zeros((WIDE, CH), F32)
        pad2[j, 65] = jnp.zeros((WIDE, CH), F32)
        for side in (2, 3):
            lines[j, side, 0:8] = jnp.zeros((8, CH), F32)
            lines[j, side, LEFT + SIDE :] = jnp.zeros((8, CH), F32)
    for dx in range(3):
        cols[dx * pairs, 0] = jnp.zeros((SIDE, CH), BF16)
        cols[dx * pairs + SIDE // 2, 1] = jnp.zeros((SIDE, CH), BF16)

    for w, wide in ((w1, wide1), (w2, wide2)):
        zero = jnp.zeros((CH, CH), BF16)
        for q in range(4):
            for dx in range(3):
                at = pl.ds((q * 3 + dx) * CH, CH)
                wide[at, 0:CH] = w[q, dx] if q < 3 else zero
                wide[at, CH : 2 * CH] = w[q - 1, dx] if q > 0 else zero

    def halo_copies(level):
        copies = []
        for k in range(8):
            copies.append(
                pltpu.make_async_remote_copy(
                    src_ref=give.at[level, k] if k < 4 else give_c.at[level, k - 4],
                    dst_ref=get.at[level, k] if k < 4 else get_c.at[level, k - 4],
                    send_sem=halo_send.at[level, k],
                    recv_sem=halo_recv.at[level, k],
                    device_id=beside(k, -1),
                    device_id_type=MESH,
                )
            )
        return copies

    def turn(level, first, strips):
        r = lax.broadcasted_iota(jnp.int32, (SIDE, SIDE), 0)
        c = lax.broadcasted_iota(jnp.int32, (SIDE, SIDE), 1)
        mirror = jnp.where(r + c == SIDE - 1, 1.0, 0.0).astype(BF16)
        turned = jnp.dot(mirror, jnp.concatenate(strips, axis=1), preferred_element_type=F32).astype(BF16)
        for s in range(len(strips)):
            pool[level, first + s] = strips[s]
            pool[level, 16 + first + s] = turned[:, s * CH : (s + 1) * CH]

    def pick(level):
        at = lax.broadcasted_iota(jnp.int32, (16, CH), 0)
        for k in range(8):
            ends = jnp.zeros((16, CH), F32)
            for j in range(TILES):
                source = table[k * 4 + asked_s[k, 4 + j, k]] + (asked_s[k, j, k] % TILES) * 4
                if k < 4:
                    give[level, k, j] = pool[level, source]
                elif k % 2 == 0:
                    ends = jnp.where(at == j, pool[level, source, SIDE - 16 :, :].astype(F32)[15:16], ends)
                else:
                    ends = jnp.where(at == j, pool[level, source, 0:16, :].astype(F32)[0:1], ends)
            if k >= 4:
                give_c[level, k - 4] = ends.astype(BF16)

    def halo_terms(level, w):
        for k in range(4):
            ends = get_c[level, k].astype(F32)
            for j in range(TILES):
                lines[j, k, LEFT : LEFT + SIDE] = get[level, k, j].astype(F32)
                at_c = LEFT - 1 if k % 2 == 0 else LEFT + SIDE
                lines[j, k // 2, at_c : at_c + 1] = ends[j : j + 1]
        sums = []
        for side, taps in enumerate((w[0], w[2], w[:, 0], w[:, 2])):
            for j in range(TILES):
                for n in range(3):
                    beyond[side, j * SIDE : (j + 1) * SIDE, n * CH : (n + 1) * CH] = lines[
                        j, side, LEFT - 1 + n : LEFT - 1 + n + SIDE
                    ].astype(BF16)
            sums.append(jnp.dot(beyond[side], taps.reshape(3 * CH, CH), preferred_element_type=F32))
        r = lax.broadcasted_iota(jnp.int32, (SIDE, CH), 0)

        def both_ends(v, first, last):
            return v + jnp.where(r == 0, first, 0.0) + jnp.where(r == SIDE - 1, last, 0.0)

        terms = []
        for j in range(TILES):
            up, low, left, right = (v[j * SIDE : (j + 1) * SIDE] for v in sums)
            terms.append((
                both_ends(up, left[0:1], right[0:1]),
                both_ends(low, left[SIDE - 1 :], right[SIDE - 1 :]),
                both_ends(left, up[0:1], low[0:1]),
                both_ends(right, up[SIDE - 1 :], low[SIDE - 1 :]),
            ))
        return terms

    def keep_edges(j, b, acc):
        @pl.when(b == 0)
        def _():
            part_row[j, 0] = acc[0, :, :CH]

        @pl.when(b == SIDE // (2 * PAIRS) - 1)
        def _():
            part_row[j, 1] = acc[PAIRS - 1, :, CH:]

        for p in range(PAIRS):
            for half in range(2):
                lanes = slice(half * CH, (half + 1) * CH)
                n = 2 * p + half
                part_col[j, 0, b, n : n + 1] = acc[p, 0:1, lanes]
                part_col[j, 1, b, n : n + 1] = acc[p, SIDE - 1 :, lanes]

    def edges(j):
        return (
            part_row[j, 0],
            part_row[j, 1],
            part_col[j, 0].reshape(SIDE, CH),
            part_col[j, 1].reshape(SIDE, CH),
        )

    def columns(j, pad, with_centre):
        def step(r, _):
            if with_centre is not None:
                centre = with_centre(r)
                pad[j, r + 1, LEFT : LEFT + SIDE, :] = centre.astype(F32)
            for dx in range(3):
                area[dx * 2 * pairs + r + 1] = pad[j, r + 1, LEFT - 1 + dx : LEFT - 1 + dx + SIDE, :].astype(BF16)
            return 0

        lax.fori_loop(0, SIDE, step, 0)

    def convolve(wide, done):
        def step(b, _):
            p = b * PAIRS
            pieces = []
            for q in range(4):
                for dx in range(3):
                    pieces.append(cols[pl.ds(p + dx * pairs + q // 2, PAIRS), q % 2].reshape(PAIRS * SIDE, CH))
            acc = jnp.dot(jnp.concatenate(pieces, axis=1), wide[...], preferred_element_type=F32)
            done(b, acc)
            return 0

        lax.fori_loop(0, SIDE // (2 * PAIRS), step, 0)

    def ring(j, pad, weight, depth):
        flat = pad.at[j].reshape(66 * WIDE, CH)
        for q in range(3):
            for dx in range(3):
                to = pl.ds((q * 3 + dx) * CH, CH)
                for s in range(4):
                    line = depth if s % 2 == 0 else SIDE - 1 - depth
                    if s < 2:
                        v = pad[j, line + q, LEFT - 1 + dx : LEFT - 1 + dx + SIDE, :]
                    else:
                        v = flat[pl.ds(q * WIDE + LEFT - 1 + line + dx, SIDE, stride=WIDE), :]
                    border[s * SIDE : (s + 1) * SIDE, to] = v.astype(BF16)
        return jnp.dot(border[...], weight, preferred_element_type=F32)

    bias1, bias2 = b1[...], b2[...]
    both1 = jnp.concatenate([bias1, bias1], axis=1)
    both2 = jnp.concatenate([bias2, bias2], axis=1)

    def whole_tile(j, _):
        all_of(j).wait_recv()

        def centre(r):
            return nested[j, pl.ds(2 * r, 2)].reshape(SIDE, CH)

        halves = nested.at[j].reshape(SIDE, 2, BLOCK, CH)
        strips = [nested[j, 0:2].reshape(SIDE, CH), nested[j, RANKS - 2 : RANKS].reshape(SIDE, CH)]
        for side in range(2):
            block = (halves[:, 1, 16:32, :] if side else halves[:, 0, 0:16, :]).astype(F32)
            flat_tmp[side] = (block[:, 8:16] if side else block[:, 0:8]).reshape(SIDE * 8, CH)
            strips.append(flat_tmp[side, pl.ds(7 * side, SIDE, stride=8), :].astype(BF16))
        turn(0, j * 4, strips)

        @pl.when(j == TILES - 1)
        def _():
            pick(0)
            for h in halo_copies(0):
                h.start()

        columns(j, pad1, centre)

        def first_done(b, acc):
            acc = (acc + both1).reshape(PAIRS, SIDE, 2 * CH)
            keep_edges(j, b, acc)
            hid = gelu(acc)
            for p in range(PAIRS):
                row = 2 * (b * PAIRS + p) + 1
                pad2[j, row, LEFT : LEFT + SIDE, :] = hid[p, :, :CH]
                pad2[j, row + 1, LEFT : LEFT + SIDE, :] = hid[p, :, CH:]

        convolve(wide1, first_done)

        @pl.when(j == TILES - 1)
        def _():
            for h in halo_copies(0):
                h.wait_recv()
            terms = halo_terms(0, w1)
            for i in range(TILES):
                flat = pad2.at[i].reshape(66 * WIDE, CH)
                hid = [gelu(part + term) for part, term in zip(edges(i), terms[i])]
                pad2[i, 1, LEFT : LEFT + SIDE, :] = hid[0]
                pad2[i, SIDE, LEFT : LEFT + SIDE, :] = hid[1]
                flat[pl.ds(WIDE + LEFT, SIDE, stride=WIDE), :] = hid[2]
                flat[pl.ds(WIDE + LEFT + SIDE - 1, SIDE, stride=WIDE), :] = hid[3]
                turn(1, i * 4, [h.astype(BF16) for h in hid])
            pick(1)
            for h in halo_copies(1):
                h.start()

        columns(j, pad2, None)

        def second_done(b, acc):
            acc = (acc + both2).reshape(PAIRS, SIDE, 2 * CH)

            @pl.when(j == TILES - 1)
            def _():
                keep_edges(j, b, acc)

            for p in range(PAIRS):
                for half in range(2):
                    row = 2 * (b * PAIRS + p) + half
                    v = acc[p, :, half * CH : (half + 1) * CH] + pad1[j, row + 1, LEFT : LEFT + SIDE, :]
                    out[j, row] = v.astype(BF16)
                    lhs[j, 0, row] = v[0:16]
                    lhs[j, 1, row] = v[SIDE - 16 :]

        convolve(wide2, second_done)
        return 0

    for a in asks:
        a.wait()
    fetch = pltpu.make_async_copy(asked, asked_s, ask_copy)
    fetch.start()
    fetch.wait()

    lax.fori_loop(0, TILES, whole_tile, 0)

    weight = w2[...].reshape(9 * CH, CH)

    def finish(i, depth, values):
        flat = pad1.at[i].reshape(66 * WIDE, CH)
        for side in (2, 3, 0, 1):
            line = depth if side % 2 == 0 else SIDE - 1 - depth
            v = values[side]
            if side < 2:
                v = v + pad1[i, line + 1, LEFT : LEFT + SIDE, :]
                lhs[i, 0, line] = v[0:16]
                lhs[i, 1, line] = v[SIDE - 16 :]
                out[i, line] = v.astype(BF16)
            else:
                v = v + flat[pl.ds(WIDE + LEFT + line, SIDE, stride=WIDE), :]
                block = lhs.at[i, side - 2].reshape(SIDE * 16, CH)
                block[pl.ds(line % 16, SIDE, stride=16), :] = v

    def rings(i, _):
        acc = ring(i, pad2, weight, 1) + bias2
        finish(i, 1, [acc[s * SIDE : (s + 1) * SIDE] for s in range(4)])
        acc = ring(i, pad2, weight, 0) + bias2
        part_row[i, 0] = acc[0:SIDE]
        part_row[i, 1] = acc[SIDE : 2 * SIDE]
        for side in range(2):
            part_col[i, side] = acc[(2 + side) * SIDE : (3 + side) * SIDE].reshape(SIDE // 16, 16, CH)
        return 0

    lax.fori_loop(0, TILES - 1, rings, 0)
    for h in halo_copies(1):
        h.wait_recv()
    terms = halo_terms(1, w2)
    for i in range(TILES):
        finish(i, 0, [part + term for part, term in zip(edges(i), terms[i])])
        out[i, :, 0:16, :] = lhs[i, 0].astype(BF16)
        out[i, :, SIDE - 16 :, :] = lhs[i, 1].astype(BF16)

    for j in range(TILES):
        all_of(j).wait_send()
    for level in range(2):
        for h in halo_copies(level):
            h.wait_send()


def shards(latitude_rows, tile_order, neighbours, rotations, w_first, b_first, w_second, b_second):
    vmem = pl.BlockSpec(memory_space=pltpu.VMEM)
    table = jnp.asarray((FLIP_TABLE * 16 + STRIP_TABLE).reshape(-1))
    dma = pltpu.SemaphoreType.DMA
    return pl.pallas_call(
        kernel,
        out_shape=jax.ShapeDtypeStruct((TILES, SIDE, SIDE, CH), BF16),
        in_specs=[pl.BlockSpec(memory_space=pltpu.HBM)] * 9,
        out_specs=vmem,
        scratch_shapes=[
            pltpu.SMEM((RANKS * TILES,), jnp.int32),
            pltpu.SMEM((32,), jnp.int32),
            pltpu.VMEM((RANKS * TILES * BLOCK // SIDE, SIDE, CH), BF16),
            pltpu.VMEM((TILES, 8), jnp.int32),
            pltpu.VMEM((TILES, 8), jnp.int32),
            pltpu.VMEM((3, 3, CH, CH), BF16),
            pltpu.VMEM((1, CH), F32),
            pltpu.VMEM((3, 3, CH, CH), BF16),
            pltpu.VMEM((1, CH), F32),
            dma((9,)),
            pltpu.VMEM((TILES, RANKS, BLOCK, CH), BF16),
            pltpu.VMEM((TILES, RANKS, BLOCK, CH), BF16),
            pltpu.VMEM((TILES, SIDE + 2, WIDE, CH), F32),
            pltpu.VMEM((TILES, SIDE + 2, WIDE, CH), F32),
            pltpu.VMEM((12 * CH, 2 * CH), BF16),
            pltpu.VMEM((12 * CH, 2 * CH), BF16),
            pltpu.VMEM((TILES, 2, SIDE, 16, CH), F32),
            pltpu.VMEM((4 * SIDE, 9 * CH), BF16),
            pltpu.VMEM((TILES, 4, WIDE, CH), F32),
            pltpu.VMEM((4, TILES * SIDE, 3 * CH), BF16),
            pltpu.VMEM((TILES, 2, SIDE, CH), F32),
            pltpu.VMEM((TILES, 2, SIDE // 16, 16, CH), F32),
            pltpu.VMEM((2, SIDE * 8, CH), F32),
            pltpu.VMEM((8, CH), jnp.int32),
            pltpu.VMEM((8, 8, CH), jnp.int32),
            pltpu.SMEM((8, 8, CH), jnp.int32),
            pltpu.VMEM((2, 32, SIDE, CH), BF16),
            pltpu.VMEM((2, 4, TILES, SIDE, CH), BF16),
            pltpu.VMEM((2, 4, TILES, SIDE, CH), BF16),
            pltpu.VMEM((2, 4, 16, CH), BF16),
            pltpu.VMEM((2, 4, 16, CH), BF16),
            dma((TILES,)),
            dma((TILES,)),
            dma((8,)),
            dma((8,)),
            dma,
            dma((2, 8)),
            dma((2, 8)),
            dma((2, 8)),
            dma((2, 8)),
        ],
        compiler_params=pltpu.CompilerParams(has_side_effects=True, vmem_limit_bytes=48 << 20),
        name="level",
    )(
        *(
            pltpu.with_memory_space_constraint(v, pltpu.HBM)
            for v in (
                tile_order, table, latitude_rows, neighbours, rotations,
                w_first, b_first.reshape(1, CH), w_second, b_second.reshape(1, CH),
            )
        )
    )


def solution(mesh):
    return jax.shard_map(
        shards,
        mesh=mesh,
        in_specs=(
            P(None, ("face", "tile"), None),
            P(),
            P(("face", "tile"), None),
            P(("face", "tile"), None),
            P(),
            P(),
            P(),
            P(),
        ),
        out_specs=P(("face", "tile"), None, None, None),
        check_vma=False,
    )
```

```python
import jax
import jax.numpy as jnp
import numpy as np
from jax import lax
from jax.experimental import pallas as pl
from jax.experimental.pallas import tpu as pltpu
from jax.sharding import PartitionSpec as P

SIDE = 64
CH = 128
TILES = 4
RANKS = 128
BLOCK = 32
WIDE = 80
LEFT = 8
PAIRS = 8
MESH = pl.DeviceIdType.MESH
BF16, F32 = jnp.bfloat16, jnp.float32

STRIP_TABLE = np.array(
    [
        [1, 2, 0, 3],
        [0, 3, 1, 2],
        [3, 1, 2, 0],
        [2, 0, 3, 1],
        [1, 2, 0, 3],
        [1, 2, 0, 3],
        [0, 3, 1, 2],
        [0, 3, 1, 2],
    ],
    np.int32,
)
FLIP_TABLE = np.array(
    [
        [0, 0, 1, 1],
        [0, 0, 1, 1],
        [0, 1, 1, 0],
        [0, 1, 1, 0],
        [0, 0, 1, 1],
        [0, 0, 1, 1],
        [0, 0, 1, 1],
        [0, 0, 1, 1],
    ],
    np.int32,
)
STEPS = ((-1, 0), (1, 0), (0, -1), (0, 1), (-1, -1), (-1, 1), (1, -1), (1, 1))


def places():
    f, t = lax.axis_index("face"), lax.axis_index("tile")
    x, c = t // 4, t % 2
    z, y = (f % 2) * 2 + (t // 2) % 2, f // 2
    xs, ys, zs = ([(v + d) % 4 for d in range(4)] for v in (x, y, z))
    cs = [c, (c + 1) % 2]
    faces = [[b * 2 + a // 2 for a in zs] for b in ys]
    tiles = [[[b * 4 + (a % 2) * 2 + e for e in cs] for a in zs] for b in xs]
    far = (2, 1, 3, 0)
    return [(faces[dy][dz], tiles[dx][dz][dc]) for dx in far for dy in far for dz in far for dc in (1, 0)]


def displaced(i):
    f, t = lax.axis_index("face"), lax.axis_index("tile")
    x, c = t // 4, t % 2
    z, y = (f % 2) * 2 + (t // 2) % 2, f // 2
    x = (x + i % 4) % 4
    y = (y + (i // 4) % 4) % 4
    z = (z + (i // 16) % 4) % 4
    c = (c + i // 64) % 2
    return y * 2 + z // 2, x * 4 + (z % 2) * 2 + c


def gelu(v):
    return 0.5 * v * (1.0 + lax.erf(v * np.float32(0.5**0.5)))


def kernel(
    order_h, table_h, lat_h, near_h, turns_h, w1_h, b1_h, w2_h, b2_h, out,
    order, table, area, near, turns, w1, b1, w2, b2, load_sem,
    sent, nested, pad1, pad2, wide1, wide2, lhs, border,
    which, near_edge, lines, beyond, part_row, part_col, flat_tmp,
    ask, asked, asked_s, pool, give, get, give_c, get_c,
    send_sem, recv_sem, ask_send, ask_recv, ask_copy, halo_send, halo_recv, corner_send, corner_recv,
):
    face, tile = lax.axis_index("face"), lax.axis_index("tile")
    me = face * 16 + tile
    lat = area.reshape(RANKS * TILES, BLOCK, CH)
    cols = area.reshape(RANKS, 2, SIDE, CH)
    pairs = SIDE // 2 + 1

    def beside(k, sign):
        df, dt = STEPS[k]
        return (face + 8 + sign * df) % 8, (tile + 16 + sign * dt) % 16

    def gather(j):
        def step(d8, _):
            for u in range(8):
                d = d8 * 8 + u
                sent[j, d] = lat[order[d * TILES + j]]
            return 0

        lax.fori_loop(0, RANKS // 8, step, 0)
        nested[j, me] = lat[order[me * TILES + j]]

    def send(j):
        def step(i, _):
            f, t = displaced((i * 37) % RANKS)
            pltpu.make_async_remote_copy(
                src_ref=sent.at[j, f * 16 + t],
                dst_ref=nested.at[j, me],
                send_sem=send_sem.at[j],
                recv_sem=recv_sem.at[j],
                device_id=(f, t),
                device_id_type=MESH,
            ).start()
            return 0

        lax.fori_loop(1, RANKS, step, 0)

    def all_of(j):
        view = nested.at[j, pl.ds(0, RANKS - 1)]
        return pltpu.make_async_remote_copy(
            src_ref=view,
            dst_ref=view,
            send_sem=send_sem.at[j],
            recv_sem=recv_sem.at[j],
            device_id=(face, tile),
            device_id_type=MESH,
        )

    loads = [
        pltpu.make_async_copy(src, dst, load_sem.at[i])
        for i, (src, dst) in enumerate((
            (order_h, order), (near_h, near), (turns_h, turns), (lat_h, lat), (table_h, table),
            (w1_h, w1), (b1_h, b1), (w2_h, w2), (b2_h, b2),
        ))
    ]
    for load in loads:
        load.start()
    ready = pltpu.get_barrier_semaphore()
    for step in places()[:-1]:
        pl.semaphore_signal(ready, inc=1, device_id=step, device_id_type=MESH)
    for load in loads[:4]:
        load.wait()
    ask[...] = jnp.zeros_like(ask)
    ask[0:4, 0:8] = near[...]
    ask[4:8, 0:8] = turns[...]
    gather(0)
    gather(1)
    pl.semaphore_wait(ready, RANKS - 1)
    asks = [
        pltpu.make_async_remote_copy(
            src_ref=ask,
            dst_ref=asked.at[k],
            send_sem=ask_send.at[k],
            recv_sem=ask_recv.at[k],
            device_id=beside(k, 1),
            device_id_type=MESH,
        )
        for k in range(8)
    ]
    for a in asks:
        a.start()

    send(0)
    gather(2)
    send(1)
    gather(3)
    send(2)
    send(3)

    for load in loads[4:]:
        load.wait()

    for pad in (pad1, pad2):
        for j in range(TILES):
            flat = pad.at[j].reshape(66 * WIDE, CH)
            for at_c in (LEFT - 1, LEFT + SIDE):
                flat[pl.ds(WIDE + at_c, SIDE, stride=WIDE), :] = jnp.zeros((SIDE, CH), F32)
    for side in range(2):
        for n in range(3):
            near_edge[side, n, 0:8] = jnp.zeros((8, CH), F32)
            near_edge[side, n, LEFT + SIDE :] = jnp.zeros((8, CH), F32)
    for j in range(TILES):
        pad2[j, 0] = jnp.zeros((WIDE, CH), F32)
        pad2[j, 65] = jnp.zeros((WIDE, CH), F32)
        for side in (2, 3):
            lines[j, side, 0:8] = jnp.zeros((8, CH), F32)
            lines[j, side, LEFT + SIDE :] = jnp.zeros((8, CH), F32)
    for dx in range(3):
        cols[dx * pairs, 0] = jnp.zeros((SIDE, CH), BF16)
        cols[dx * pairs + SIDE // 2, 1] = jnp.zeros((SIDE, CH), BF16)

    for w, wide in ((w1, wide1), (w2, wide2)):
        zero = jnp.zeros((CH, CH), BF16)
        for q in range(4):
            for dx in range(3):
                at = pl.ds((q * 3 + dx) * CH, CH)
                wide[at, 0:CH] = w[q, dx] if q < 3 else zero
                wide[at, CH : 2 * CH] = w[q - 1, dx] if q > 0 else zero

    def halo_copies(level):
        copies = []
        for k in (4, 5, 6, 7, 0, 1, 2, 3):
            copies.append(
                pltpu.make_async_remote_copy(
                    src_ref=give.at[level, k] if k < 4 else give_c.at[level, k - 4],
                    dst_ref=get.at[level, k] if k < 4 else get_c.at[level, k - 4],
                    send_sem=halo_send.at[level, k],
                    recv_sem=halo_recv.at[level, k],
                    device_id=beside(k, -1),
                    device_id_type=MESH,
                )
            )
        return copies

    def turn(level, first, strips):
        r = lax.broadcasted_iota(jnp.int32, (SIDE, SIDE), 0)
        c = lax.broadcasted_iota(jnp.int32, (SIDE, SIDE), 1)
        mirror = jnp.where(r + c == SIDE - 1, 1.0, 0.0).astype(BF16)
        turned = jnp.dot(mirror, jnp.concatenate(strips, axis=1), preferred_element_type=F32).astype(BF16)
        for s in range(len(strips)):
            pool[level, first + s] = strips[s]
            pool[level, 16 + first + s] = turned[:, s * CH : (s + 1) * CH]

    def pick(level):
        at = lax.broadcasted_iota(jnp.int32, (16, CH), 0)
        for k in (4, 5, 6, 7, 0, 1, 2, 3):
            ends = jnp.zeros((16, CH), F32)
            for j in range(TILES):
                source = which[k * TILES + j]
                if k < 4:
                    give[level, k, j] = pool[level, source]
                elif k % 2 == 0:
                    ends = jnp.where(at == j, pool[level, source, SIDE - 16 :, :].astype(F32)[15:16], ends)
                else:
                    ends = jnp.where(at == j, pool[level, source, 0:16, :].astype(F32)[0:1], ends)
            if k >= 4:
                give_c[level, k - 4] = ends.astype(BF16)

    def halo_terms(level, w):
        for k in range(4):
            ends = get_c[level, k].astype(F32)
            for j in range(TILES):
                lines[j, k, LEFT : LEFT + SIDE] = get[level, k, j].astype(F32)
                at_c = LEFT - 1 if k % 2 == 0 else LEFT + SIDE
                lines[j, k // 2, at_c : at_c + 1] = ends[j : j + 1]
        sums = []
        for side, taps in enumerate((w[0], w[2], w[:, 0], w[:, 2])):
            for j in range(TILES):
                for n in range(3):
                    beyond[side, j * SIDE : (j + 1) * SIDE, n * CH : (n + 1) * CH] = lines[
                        j, side, LEFT - 1 + n : LEFT - 1 + n + SIDE
                    ].astype(BF16)
            sums.append(jnp.dot(beyond[side], taps.reshape(3 * CH, CH), preferred_element_type=F32))
        r = lax.broadcasted_iota(jnp.int32, (SIDE, CH), 0)

        def both_ends(v, first, last):
            return v + jnp.where(r == 0, first, 0.0) + jnp.where(r == SIDE - 1, last, 0.0)

        terms = []
        for j in range(TILES):
            up, low, left, right = (v[j * SIDE : (j + 1) * SIDE] for v in sums)
            terms.append((
                both_ends(up, left[0:1], right[0:1]),
                both_ends(low, left[SIDE - 1 :], right[SIDE - 1 :]),
                both_ends(left, up[0:1], low[0:1]),
                both_ends(right, up[SIDE - 1 :], low[SIDE - 1 :]),
            ))
        return terms

    def keep_edges(j, b, acc):
        @pl.when(b == 0)
        def _():
            part_row[j, 0] = acc[0, :, :CH]

        @pl.when(b == SIDE // (2 * PAIRS) - 1)
        def _():
            part_row[j, 1] = acc[PAIRS - 1, :, CH:]

        for p in range(PAIRS):
            for half in range(2):
                lanes = slice(half * CH, (half + 1) * CH)
                n = 2 * p + half
                part_col[j, 0, b, n : n + 1] = acc[p, 0:1, lanes]
                part_col[j, 1, b, n : n + 1] = acc[p, SIDE - 1 :, lanes]

    def edges(j):
        return (
            part_row[j, 0],
            part_row[j, 1],
            part_col[j, 0].reshape(SIDE, CH),
            part_col[j, 1].reshape(SIDE, CH),
        )

    def columns(j, pad, with_centre):
        def step(r, _):
            if with_centre is not None:
                centre = with_centre(r)
                pad[j, r + 1, LEFT : LEFT + SIDE, :] = centre.astype(F32)
            for dx in range(3):
                area[dx * 2 * pairs + r + 1] = pad[j, r + 1, LEFT - 1 + dx : LEFT - 1 + dx + SIDE, :].astype(BF16)
            return 0

        lax.fori_loop(0, SIDE, step, 0)

    def convolve(wide, done):
        def step(b, _):
            p = b * PAIRS
            pieces = []
            for q in range(4):
                for dx in range(3):
                    pieces.append(cols[pl.ds(p + dx * pairs + q // 2, PAIRS), q % 2].reshape(PAIRS * SIDE, CH))
            acc = jnp.dot(jnp.concatenate(pieces, axis=1), wide[...], preferred_element_type=F32)
            done(b, acc)
            return 0

        lax.fori_loop(0, SIDE // (2 * PAIRS), step, 0)

    def ring(j, pad, weight):
        flat = pad.at[j].reshape(66 * WIDE, CH)
        for side in range(2):
            for n in range(3):
                c = SIDE - 1 - n if side else n
                near_edge[side, n, LEFT : LEFT + SIDE] = flat[pl.ds(WIDE + LEFT + c, SIDE, stride=WIDE), :]
        for depth in range(2):
            for s in range(4):
                at = slice((depth * 4 + s) * SIDE, (depth * 4 + s + 1) * SIDE)
                line = depth if s % 2 == 0 else SIDE - 1 - depth
                for q in range(3):
                    for dx in range(3):
                        n = depth + (dx - 1 if s == 2 else 1 - dx)
                        if s < 2:
                            v = pad[j, line + q, LEFT - 1 + dx : LEFT - 1 + dx + SIDE, :].astype(BF16)
                        elif n < 0:
                            v = jnp.zeros((SIDE, CH), BF16)
                        else:
                            v = near_edge[s - 2, n, LEFT - 1 + q : LEFT - 1 + q + SIDE].astype(BF16)
                        border[at, (q * 3 + dx) * CH : (q * 3 + dx + 1) * CH] = v
        return jnp.dot(border[...], weight, preferred_element_type=F32)

    bias1, bias2 = b1[...], b2[...]
    both1 = jnp.concatenate([bias1, bias1], axis=1)
    both2 = jnp.concatenate([bias2, bias2], axis=1)

    def whole_tile(j, _):
        all_of(j).wait_recv()

        def centre(r):
            return nested[j, pl.ds(2 * r, 2)].reshape(SIDE, CH)

        halves = nested.at[j].reshape(SIDE, 2, BLOCK, CH)
        strips = [nested[j, 0:2].reshape(SIDE, CH), nested[j, RANKS - 2 : RANKS].reshape(SIDE, CH)]
        for side in range(2):
            block = (halves[:, 1, 16:32, :] if side else halves[:, 0, 0:16, :]).astype(F32)
            flat_tmp[side] = (block[:, 8:16] if side else block[:, 0:8]).reshape(SIDE * 8, CH)
            strips.append(flat_tmp[side, pl.ds(7 * side, SIDE, stride=8), :].astype(BF16))
        turn(0, j * 4, strips)

        @pl.when(j == TILES - 1)
        def _():
            pick(0)
            for h in halo_copies(0):
                h.start()

        columns(j, pad1, centre)

        def first_done(b, acc):
            acc = (acc + both1).reshape(PAIRS, SIDE, 2 * CH)
            keep_edges(j, b, acc)
            hid = gelu(acc)
            for p in range(PAIRS):
                row = 2 * (b * PAIRS + p) + 1
                pad2[j, row, LEFT : LEFT + SIDE, :] = hid[p, :, :CH]
                pad2[j, row + 1, LEFT : LEFT + SIDE, :] = hid[p, :, CH:]

        convolve(wide1, first_done)

        @pl.when(j == TILES - 1)
        def _():
            for h in halo_copies(0):
                h.wait_recv()
            terms = halo_terms(0, w1)
            for i in range(TILES):
                turn(1, i * 4, [gelu(part + term).astype(BF16) for part, term in zip(edges(i), terms[i])])
            pick(1)
            for h in halo_copies(1):
                h.start()
            for i in range(TILES):
                flat = pad2.at[i].reshape(66 * WIDE, CH)
                pad2[i, 1, LEFT : LEFT + SIDE, :] = pool[1, i * 4].astype(F32)
                pad2[i, SIDE, LEFT : LEFT + SIDE, :] = pool[1, i * 4 + 1].astype(F32)
                flat[pl.ds(WIDE + LEFT, SIDE, stride=WIDE), :] = pool[1, i * 4 + 2].astype(F32)
                flat[pl.ds(WIDE + LEFT + SIDE - 1, SIDE, stride=WIDE), :] = pool[1, i * 4 + 3].astype(F32)

        columns(j, pad2, None)

        def second_done(b, acc):
            acc = (acc + both2).reshape(PAIRS, SIDE, 2 * CH)

            @pl.when(j == TILES - 1)
            def _():
                keep_edges(j, b, acc)

            for p in range(PAIRS):
                for half in range(2):
                    row = 2 * (b * PAIRS + p) + half
                    v = acc[p, :, half * CH : (half + 1) * CH] + pad1[j, row + 1, LEFT : LEFT + SIDE, :]
                    out[j, row] = v.astype(BF16)
                    lhs[j, 0, row] = v[0:16]
                    lhs[j, 1, row] = v[SIDE - 16 :]

        convolve(wide2, second_done)
        return 0

    for a in asks:
        a.wait()
    fetch = pltpu.make_async_copy(asked, asked_s, ask_copy)
    fetch.start()
    fetch.wait()
    for k in range(8):
        for j in range(TILES):
            which[k * TILES + j] = table[k * 4 + asked_s[k, 4 + j, k]] + (asked_s[k, j, k] % TILES) * 4

    lax.fori_loop(0, TILES, whole_tile, 0)

    weight = w2[...].reshape(9 * CH, CH)

    def finish(i, depth, values):
        flat = pad1.at[i].reshape(66 * WIDE, CH)
        for side in (2, 3, 0, 1):
            line = depth if side % 2 == 0 else SIDE - 1 - depth
            v = values[side]
            if side < 2:
                v = v + pad1[i, line + 1, LEFT : LEFT + SIDE, :]
                lhs[i, 0, line] = v[0:16]
                lhs[i, 1, line] = v[SIDE - 16 :]
                out[i, line] = v.astype(BF16)
            else:
                v = v + flat[pl.ds(WIDE + LEFT + line, SIDE, stride=WIDE), :]
                block = lhs.at[i, side - 2].reshape(SIDE * 16, CH)
                block[pl.ds(line % 16, SIDE, stride=16), :] = v

    def rings(i, _):
        acc = ring(i, pad2, weight) + bias2
        finish(i, 1, [acc[(4 + s) * SIDE : (5 + s) * SIDE] for s in range(4)])
        part_row[i, 0] = acc[0:SIDE]
        part_row[i, 1] = acc[SIDE : 2 * SIDE]
        for side in range(2):
            part_col[i, side] = acc[(2 + side) * SIDE : (3 + side) * SIDE].reshape(SIDE // 16, 16, CH)
        return 0

    lax.fori_loop(0, TILES - 1, rings, 0)
    for h in halo_copies(1):
        h.wait_recv()
    terms = halo_terms(1, w2)
    for i in range(TILES):
        finish(i, 0, [part + term for part, term in zip(edges(i), terms[i])])
        out[i, :, 0:16, :] = lhs[i, 0].astype(BF16)
        out[i, :, SIDE - 16 :, :] = lhs[i, 1].astype(BF16)

    for j in range(TILES):
        all_of(j).wait_send()
    for level in range(2):
        for h in halo_copies(level):
            h.wait_send()


def shards(latitude_rows, tile_order, neighbours, rotations, w_first, b_first, w_second, b_second):
    vmem = pl.BlockSpec(memory_space=pltpu.VMEM)
    table = jnp.asarray((FLIP_TABLE * 16 + STRIP_TABLE).reshape(-1))
    dma = pltpu.SemaphoreType.DMA
    return pl.pallas_call(
        kernel,
        out_shape=jax.ShapeDtypeStruct((TILES, SIDE, SIDE, CH), BF16),
        in_specs=[pl.BlockSpec(memory_space=pltpu.HBM)] * 9,
        out_specs=vmem,
        scratch_shapes=[
            pltpu.SMEM((RANKS * TILES,), jnp.int32),
            pltpu.SMEM((32,), jnp.int32),
            pltpu.VMEM((RANKS * TILES * BLOCK // SIDE, SIDE, CH), BF16),
            pltpu.VMEM((TILES, 8), jnp.int32),
            pltpu.VMEM((TILES, 8), jnp.int32),
            pltpu.VMEM((3, 3, CH, CH), BF16),
            pltpu.VMEM((1, CH), F32),
            pltpu.VMEM((3, 3, CH, CH), BF16),
            pltpu.VMEM((1, CH), F32),
            dma((9,)),
            pltpu.VMEM((TILES, RANKS, BLOCK, CH), BF16),
            pltpu.VMEM((TILES, RANKS, BLOCK, CH), BF16),
            pltpu.VMEM((TILES, SIDE + 2, WIDE, CH), F32),
            pltpu.VMEM((TILES, SIDE + 2, WIDE, CH), F32),
            pltpu.VMEM((12 * CH, 2 * CH), BF16),
            pltpu.VMEM((12 * CH, 2 * CH), BF16),
            pltpu.VMEM((TILES, 2, SIDE, 16, CH), F32),
            pltpu.VMEM((8 * SIDE, 9 * CH), BF16),
            pltpu.SMEM((8 * TILES,), jnp.int32),
            pltpu.VMEM((2, 3, WIDE, CH), F32),
            pltpu.VMEM((TILES, 4, WIDE, CH), F32),
            pltpu.VMEM((4, TILES * SIDE, 3 * CH), BF16),
            pltpu.VMEM((TILES, 2, SIDE, CH), F32),
            pltpu.VMEM((TILES, 2, SIDE // 16, 16, CH), F32),
            pltpu.VMEM((2, SIDE * 8, CH), F32),
            pltpu.VMEM((8, CH), jnp.int32),
            pltpu.VMEM((8, 8, CH), jnp.int32),
            pltpu.SMEM((8, 8, CH), jnp.int32),
            pltpu.VMEM((2, 32, SIDE, CH), BF16),
            pltpu.VMEM((2, 4, TILES, SIDE, CH), BF16),
            pltpu.VMEM((2, 4, TILES, SIDE, CH), BF16),
            pltpu.VMEM((2, 4, 16, CH), BF16),
            pltpu.VMEM((2, 4, 16, CH), BF16),
            dma((TILES,)),
            dma((TILES,)),
            dma((8,)),
            dma((8,)),
            dma,
            dma((2, 8)),
            dma((2, 8)),
            dma((2, 8)),
            dma((2, 8)),
        ],
        compiler_params=pltpu.CompilerParams(collective_id=0, has_side_effects=True, vmem_limit_bytes=48 << 20),
        name="level",
    )(
        *(
            pltpu.with_memory_space_constraint(v, pltpu.HBM)
            for v in (
                tile_order, table, latitude_rows, neighbours, rotations,
                w_first, b_first.reshape(1, CH), w_second, b_second.reshape(1, CH),
            )
        )
    )


def solution(mesh):
    return jax.shard_map(
        shards,
        mesh=mesh,
        in_specs=(
            P(None, ("face", "tile"), None),
            P(),
            P(("face", "tile"), None),
            P(("face", "tile"), None),
            P(),
            P(),
            P(),
            P(),
        ),
        out_specs=P(("face", "tile"), None, None, None),
        check_vma=False,
    )
```

```python
import jax
import jax.numpy as jnp
import numpy as np
from jax import lax
from jax.experimental import pallas as pl
from jax.experimental.pallas import tpu as pltpu
from jax.sharding import PartitionSpec as P

SIDE = 64
CH = 128
TILES = 4
RANKS = 128
BLOCK = 32
WIDE = 80
LEFT = 8
PAIRS = 8
MESH = pl.DeviceIdType.MESH
BF16, F32 = jnp.bfloat16, jnp.float32

STRIP_TABLE = np.array(
    [
        [1, 2, 0, 3],
        [0, 3, 1, 2],
        [3, 1, 2, 0],
        [2, 0, 3, 1],
        [1, 2, 0, 3],
        [1, 2, 0, 3],
        [0, 3, 1, 2],
        [0, 3, 1, 2],
    ],
    np.int32,
)
FLIP_TABLE = np.array(
    [
        [0, 0, 1, 1],
        [0, 0, 1, 1],
        [0, 1, 1, 0],
        [0, 1, 1, 0],
        [0, 0, 1, 1],
        [0, 0, 1, 1],
        [0, 0, 1, 1],
        [0, 0, 1, 1],
    ],
    np.int32,
)
STEPS = ((-1, 0), (1, 0), (0, -1), (0, 1), (-1, -1), (-1, 1), (1, -1), (1, 1))


def places():
    f, t = lax.axis_index("face"), lax.axis_index("tile")
    x, c = t // 4, t % 2
    z, y = (f % 2) * 2 + (t // 2) % 2, f // 2
    xs, ys, zs = ([(v + d) % 4 for d in range(4)] for v in (x, y, z))
    cs = [c, (c + 1) % 2]
    faces = [[b * 2 + a // 2 for a in zs] for b in ys]
    tiles = [[[b * 4 + (a % 2) * 2 + e for e in cs] for a in zs] for b in xs]
    far = (2, 1, 3, 0)
    return [(faces[dy][dz], tiles[dx][dz][dc]) for dx in far for dy in far for dz in far for dc in (1, 0)]


def displaced(i):
    f, t = lax.axis_index("face"), lax.axis_index("tile")
    x, c = t // 4, t % 2
    z, y = (f % 2) * 2 + (t // 2) % 2, f // 2
    x = (x + i % 4) % 4
    y = (y + (i // 4) % 4) % 4
    z = (z + (i // 16) % 4) % 4
    c = (c + i // 64) % 2
    return y * 2 + z // 2, x * 4 + (z % 2) * 2 + c


def gelu(v):
    return 0.5 * v * (1.0 + lax.erf(v * np.float32(0.5**0.5)))


def kernel(
    order_h, table_h, lat_h, near_h, turns_h, w1_h, b1_h, w2_h, b2_h, out,
    order, table, area, near, turns, w1, b1, w2, b2, load_sem,
    sent, nested, pad1, pad2, wide1, wide2, lhs, border,
    which, near_edge, lines, beyond, part_row, part_col, flat_tmp,
    ask, asked, asked_s, pool, give, get, give_c, get_c,
    send_sem, recv_sem, ask_send, ask_recv, ask_copy, halo_send, halo_recv, corner_send, corner_recv,
):
    face, tile = lax.axis_index("face"), lax.axis_index("tile")
    me = face * 16 + tile
    lat = area.reshape(RANKS * TILES, BLOCK, CH)
    cols = area.reshape(RANKS, 2, SIDE, CH)
    pairs = SIDE // 2 + 1

    def beside(k, sign):
        df, dt = STEPS[k]
        return (face + 8 + sign * df) % 8, (tile + 16 + sign * dt) % 16

    def gather(j):
        def step(d8, _):
            for u in range(8):
                d = d8 * 8 + u
                sent[j, d] = lat[order[d * TILES + j]]
            return 0

        lax.fori_loop(0, RANKS // 8, step, 0)
        nested[j, me] = lat[order[me * TILES + j]]

    def send(j):
        def step(i, _):
            f, t = displaced((i * 37) % RANKS)
            pltpu.make_async_remote_copy(
                src_ref=sent.at[j, f * 16 + t],
                dst_ref=nested.at[j, me],
                send_sem=send_sem.at[j],
                recv_sem=recv_sem.at[j],
                device_id=(f, t),
                device_id_type=MESH,
            ).start()
            return 0

        lax.fori_loop(1, RANKS, step, 0)

    def all_of(j):
        view = nested.at[j, pl.ds(0, RANKS - 1)]
        return pltpu.make_async_remote_copy(
            src_ref=view,
            dst_ref=view,
            send_sem=send_sem.at[j],
            recv_sem=recv_sem.at[j],
            device_id=(face, tile),
            device_id_type=MESH,
        )

    quarters = [pl.ds(q * RANKS, RANKS) for q in range(4)]
    loads = [
        pltpu.make_async_copy(src, dst, load_sem.at[i])
        for i, (src, dst) in enumerate((
            (order_h, order), (near_h, near), (turns_h, turns),
            *((lat_h.at[q], lat.at[q]) for q in quarters), (table_h, table),
            (w1_h, w1), (b1_h, b1), (w2_h, w2), (b2_h, b2),
        ))
    ]
    for load in loads:
        load.start()
    ready = pltpu.get_barrier_semaphore()
    for step in places()[:-1]:
        pl.semaphore_signal(ready, inc=1, device_id=step, device_id_type=MESH)
    for load in loads[:7]:
        load.wait()
    ask[...] = jnp.zeros_like(ask)
    ask[0:4, 0:8] = near[...]
    ask[4:8, 0:8] = turns[...]
    gather(0)
    gather(1)
    pl.semaphore_wait(ready, RANKS - 1)
    asks = [
        pltpu.make_async_remote_copy(
            src_ref=ask,
            dst_ref=asked.at[k],
            send_sem=ask_send.at[k],
            recv_sem=ask_recv.at[k],
            device_id=beside(k, 1),
            device_id_type=MESH,
        )
        for k in range(8)
    ]
    for a in asks:
        a.start()

    send(0)
    gather(2)
    send(1)
    gather(3)
    send(2)
    send(3)

    for load in loads[7:]:
        load.wait()

    for pad in (pad1, pad2):
        for j in range(TILES):
            flat = pad.at[j].reshape(66 * WIDE, CH)
            for at_c in (LEFT - 1, LEFT + SIDE):
                flat[pl.ds(WIDE + at_c, SIDE, stride=WIDE), :] = jnp.zeros((SIDE, CH), F32)
    for side in range(2):
        for n in range(3):
            near_edge[side, n, 0:8] = jnp.zeros((8, CH), F32)
            near_edge[side, n, LEFT + SIDE :] = jnp.zeros((8, CH), F32)
    for j in range(TILES):
        pad2[j, 0] = jnp.zeros((WIDE, CH), F32)
        pad2[j, 65] = jnp.zeros((WIDE, CH), F32)
        for side in (2, 3):
            lines[j, side, 0:8] = jnp.zeros((8, CH), F32)
            lines[j, side, LEFT + SIDE :] = jnp.zeros((8, CH), F32)
    for dx in range(3):
        cols[dx * pairs, 0] = jnp.zeros((SIDE, CH), BF16)
        cols[dx * pairs + SIDE // 2, 1] = jnp.zeros((SIDE, CH), BF16)

    for w, wide in ((w1, wide1), (w2, wide2)):
        zero = jnp.zeros((CH, CH), BF16)
        for q in range(4):
            for dx in range(3):
                at = pl.ds((q * 3 + dx) * CH, CH)
                wide[at, 0:CH] = w[q, dx] if q < 3 else zero
                wide[at, CH : 2 * CH] = w[q - 1, dx] if q > 0 else zero

    def halo_copies(level):
        copies = []
        for k in (4, 5, 6, 7, 0, 1, 2, 3):
            copies.append(
                pltpu.make_async_remote_copy(
                    src_ref=give.at[level, k] if k < 4 else give_c.at[level, k - 4],
                    dst_ref=get.at[level, k] if k < 4 else get_c.at[level, k - 4],
                    send_sem=halo_send.at[level, k],
                    recv_sem=halo_recv.at[level, k],
                    device_id=beside(k, -1),
                    device_id_type=MESH,
                )
            )
        return copies

    def turn(level, first, strips):
        r = lax.broadcasted_iota(jnp.int32, (SIDE, SIDE), 0)
        c = lax.broadcasted_iota(jnp.int32, (SIDE, SIDE), 1)
        mirror = jnp.where(r + c == SIDE - 1, 1.0, 0.0).astype(BF16)
        turned = jnp.dot(mirror, jnp.concatenate(strips, axis=1), preferred_element_type=F32).astype(BF16)
        for s in range(len(strips)):
            pool[level, first + s] = strips[s]
            pool[level, 16 + first + s] = turned[:, s * CH : (s + 1) * CH]

    def pick(level):
        at = lax.broadcasted_iota(jnp.int32, (16, CH), 0)
        for k in (4, 5, 6, 7, 0, 1, 2, 3):
            ends = jnp.zeros((16, CH), F32)
            for j in range(TILES):
                source = which[k * TILES + j]
                if k < 4:
                    give[level, k, j] = pool[level, source]
                elif k % 2 == 0:
                    ends = jnp.where(at == j, pool[level, source, SIDE - 16 :, :].astype(F32)[15:16], ends)
                else:
                    ends = jnp.where(at == j, pool[level, source, 0:16, :].astype(F32)[0:1], ends)
            if k >= 4:
                give_c[level, k - 4] = ends.astype(BF16)

    def halo_terms(level, w):
        copies = halo_copies(level)
        sums = [None] * 4
        for side in (2, 3, 0, 1):
            if side == 0:
                for k in range(4):
                    copies[k].wait_recv()
                    ends = get_c[level, k].astype(F32)
                    at_c = LEFT - 1 if k % 2 == 0 else LEFT + SIDE
                    for j in range(TILES):
                        lines[j, k // 2, at_c : at_c + 1] = ends[j : j + 1]
            copies[4 + side].wait_recv()
            taps = (w[0], w[2], w[:, 0], w[:, 2])[side].reshape(3 * CH, CH)
            for j in range(TILES):
                lines[j, side, LEFT : LEFT + SIDE] = get[level, side, j].astype(F32)
                for n in range(3):
                    beyond[side, j * SIDE : (j + 1) * SIDE, n * CH : (n + 1) * CH] = lines[
                        j, side, LEFT - 1 + n : LEFT - 1 + n + SIDE
                    ].astype(BF16)
            sums[side] = jnp.dot(beyond[side], taps, preferred_element_type=F32)
        r = lax.broadcasted_iota(jnp.int32, (SIDE, CH), 0)

        def both_ends(v, first, last):
            return v + jnp.where(r == 0, first, 0.0) + jnp.where(r == SIDE - 1, last, 0.0)

        terms = []
        for j in range(TILES):
            up, low, left, right = (v[j * SIDE : (j + 1) * SIDE] for v in sums)
            terms.append((
                both_ends(up, left[0:1], right[0:1]),
                both_ends(low, left[SIDE - 1 :], right[SIDE - 1 :]),
                both_ends(left, up[0:1], low[0:1]),
                both_ends(right, up[SIDE - 1 :], low[SIDE - 1 :]),
            ))
        return terms

    def keep_edges(j, b, acc):
        @pl.when(b == 0)
        def _():
            part_row[j, 0] = acc[0, :, :CH]

        @pl.when(b == SIDE // (2 * PAIRS) - 1)
        def _():
            part_row[j, 1] = acc[PAIRS - 1, :, CH:]

        for p in range(PAIRS):
            for half in range(2):
                lanes = slice(half * CH, (half + 1) * CH)
                n = 2 * p + half
                part_col[j, 0, b, n : n + 1] = acc[p, 0:1, lanes]
                part_col[j, 1, b, n : n + 1] = acc[p, SIDE - 1 :, lanes]

    def edges(j):
        return (
            part_row[j, 0],
            part_row[j, 1],
            part_col[j, 0].reshape(SIDE, CH),
            part_col[j, 1].reshape(SIDE, CH),
        )

    def columns(j, pad, with_centre):
        def step(r, _):
            if with_centre is not None:
                centre = with_centre(r)
                pad[j, r + 1, LEFT : LEFT + SIDE, :] = centre.astype(F32)
            for dx in range(3):
                area[dx * 2 * pairs + r + 1] = pad[j, r + 1, LEFT - 1 + dx : LEFT - 1 + dx + SIDE, :].astype(BF16)
            return 0

        lax.fori_loop(0, SIDE, step, 0)

    def convolve(wide, done):
        def step(b, _):
            p = b * PAIRS
            pieces = []
            for q in range(4):
                for dx in range(3):
                    pieces.append(cols[pl.ds(p + dx * pairs + q // 2, PAIRS), q % 2].reshape(PAIRS * SIDE, CH))
            acc = jnp.dot(jnp.concatenate(pieces, axis=1), wide[...], preferred_element_type=F32)
            done(b, acc)
            return 0

        lax.fori_loop(0, SIDE // (2 * PAIRS), step, 0)

    def ring(j, pad, weight):
        flat = pad.at[j].reshape(66 * WIDE, CH)
        for side in range(2):
            for n in range(3):
                c = SIDE - 1 - n if side else n
                near_edge[side, n, LEFT : LEFT + SIDE] = flat[pl.ds(WIDE + LEFT + c, SIDE, stride=WIDE), :]
        for depth in range(2):
            for s in range(4):
                at = slice((depth * 4 + s) * SIDE, (depth * 4 + s + 1) * SIDE)
                line = depth if s % 2 == 0 else SIDE - 1 - depth
                for q in range(3):
                    for dx in range(3):
                        n = depth + (dx - 1 if s == 2 else 1 - dx)
                        if s < 2:
                            v = pad[j, line + q, LEFT - 1 + dx : LEFT - 1 + dx + SIDE, :].astype(BF16)
                        elif n < 0:
                            v = jnp.zeros((SIDE, CH), BF16)
                        else:
                            v = near_edge[s - 2, n, LEFT - 1 + q : LEFT - 1 + q + SIDE].astype(BF16)
                        border[at, (q * 3 + dx) * CH : (q * 3 + dx + 1) * CH] = v
        return jnp.dot(border[...], weight, preferred_element_type=F32)

    bias1, bias2 = b1[...], b2[...]
    both1 = jnp.concatenate([bias1, bias1], axis=1)
    both2 = jnp.concatenate([bias2, bias2], axis=1)

    def whole_tile(j, _):
        all_of(j).wait_recv()

        def centre(r):
            return nested[j, pl.ds(2 * r, 2)].reshape(SIDE, CH)

        halves = nested.at[j].reshape(SIDE, 2, BLOCK, CH)
        strips = [nested[j, 0:2].reshape(SIDE, CH), nested[j, RANKS - 2 : RANKS].reshape(SIDE, CH)]
        for side in range(2):
            block = (halves[:, 1, 16:32, :] if side else halves[:, 0, 0:16, :]).astype(F32)
            flat_tmp[side] = (block[:, 8:16] if side else block[:, 0:8]).reshape(SIDE * 8, CH)
            strips.append(flat_tmp[side, pl.ds(7 * side, SIDE, stride=8), :].astype(BF16))
        turn(0, j * 4, strips)

        @pl.when(j == TILES - 1)
        def _():
            pick(0)
            for h in halo_copies(0):
                h.start()

        columns(j, pad1, centre)

        def first_done(b, acc):
            acc = (acc + both1).reshape(PAIRS, SIDE, 2 * CH)
            keep_edges(j, b, acc)
            hid = gelu(acc)
            for p in range(PAIRS):
                row = 2 * (b * PAIRS + p) + 1
                pad2[j, row, LEFT : LEFT + SIDE, :] = hid[p, :, :CH]
                pad2[j, row + 1, LEFT : LEFT + SIDE, :] = hid[p, :, CH:]

        convolve(wide1, first_done)

        @pl.when(j == TILES - 1)
        def _():
            terms = halo_terms(0, w1)
            for i in range(TILES):
                turn(1, i * 4, [gelu(part + term).astype(BF16) for part, term in zip(edges(i), terms[i])])
            pick(1)
            for h in halo_copies(1):
                h.start()
            for i in range(TILES):
                flat = pad2.at[i].reshape(66 * WIDE, CH)
                pad2[i, 1, LEFT : LEFT + SIDE, :] = pool[1, i * 4].astype(F32)
                pad2[i, SIDE, LEFT : LEFT + SIDE, :] = pool[1, i * 4 + 1].astype(F32)
                flat[pl.ds(WIDE + LEFT, SIDE, stride=WIDE), :] = pool[1, i * 4 + 2].astype(F32)
                flat[pl.ds(WIDE + LEFT + SIDE - 1, SIDE, stride=WIDE), :] = pool[1, i * 4 + 3].astype(F32)

        columns(j, pad2, None)

        def second_done(b, acc):
            acc = (acc + both2).reshape(PAIRS, SIDE, 2 * CH)

            @pl.when(j == TILES - 1)
            def _():
                keep_edges(j, b, acc)

            for p in range(PAIRS):
                for half in range(2):
                    row = 2 * (b * PAIRS + p) + half
                    v = acc[p, :, half * CH : (half + 1) * CH] + pad1[j, row + 1, LEFT : LEFT + SIDE, :]
                    out[j, row] = v.astype(BF16)
                    lhs[j, 0, row] = v[0:16]
                    lhs[j, 1, row] = v[SIDE - 16 :]

        convolve(wide2, second_done)
        return 0

    for a in asks:
        a.wait()
    fetch = pltpu.make_async_copy(asked, asked_s, ask_copy)
    fetch.start()
    fetch.wait()
    for k in range(8):
        for j in range(TILES):
            which[k * TILES + j] = table[k * 4 + asked_s[k, 4 + j, k]] + (asked_s[k, j, k] % TILES) * 4

    lax.fori_loop(0, TILES, whole_tile, 0)

    weight = w2[...].reshape(9 * CH, CH)

    def finish(i, depth, values):
        flat = pad1.at[i].reshape(66 * WIDE, CH)
        for side in (2, 3, 0, 1):
            line = depth if side % 2 == 0 else SIDE - 1 - depth
            v = values[side]
            if side < 2:
                v = v + pad1[i, line + 1, LEFT : LEFT + SIDE, :]
                lhs[i, 0, line] = v[0:16]
                lhs[i, 1, line] = v[SIDE - 16 :]
                out[i, line] = v.astype(BF16)
            else:
                v = v + flat[pl.ds(WIDE + LEFT + line, SIDE, stride=WIDE), :]
                block = lhs.at[i, side - 2].reshape(SIDE * 16, CH)
                block[pl.ds(line % 16, SIDE, stride=16), :] = v

    def rings(i, _):
        acc = ring(i, pad2, weight) + bias2
        finish(i, 1, [acc[(4 + s) * SIDE : (5 + s) * SIDE] for s in range(4)])
        part_row[i, 0] = acc[0:SIDE]
        part_row[i, 1] = acc[SIDE : 2 * SIDE]
        for side in range(2):
            part_col[i, side] = acc[(2 + side) * SIDE : (3 + side) * SIDE].reshape(SIDE // 16, 16, CH)
        return 0

    lax.fori_loop(0, TILES - 1, rings, 0)
    terms = halo_terms(1, w2)
    for i in range(TILES):
        finish(i, 0, [part + term for part, term in zip(edges(i), terms[i])])
        out[i, :, 0:16, :] = lhs[i, 0].astype(BF16)
        out[i, :, SIDE - 16 :, :] = lhs[i, 1].astype(BF16)

    for j in range(TILES):
        all_of(j).wait_send()
    for level in range(2):
        for h in halo_copies(level):
            h.wait_send()


def shards(latitude_rows, tile_order, neighbours, rotations, w_first, b_first, w_second, b_second):
    vmem = pl.BlockSpec(memory_space=pltpu.VMEM)
    table = jnp.asarray((FLIP_TABLE * 16 + STRIP_TABLE).reshape(-1))
    dma = pltpu.SemaphoreType.DMA
    return pl.pallas_call(
        kernel,
        out_shape=jax.ShapeDtypeStruct((TILES, SIDE, SIDE, CH), BF16),
        in_specs=[pl.BlockSpec(memory_space=pltpu.HBM)] * 9,
        out_specs=vmem,
        scratch_shapes=[
            pltpu.SMEM((RANKS * TILES,), jnp.int32),
            pltpu.SMEM((32,), jnp.int32),
            pltpu.VMEM((RANKS * TILES * BLOCK // SIDE, SIDE, CH), BF16),
            pltpu.VMEM((TILES, 8), jnp.int32),
            pltpu.VMEM((TILES, 8), jnp.int32),
            pltpu.VMEM((3, 3, CH, CH), BF16),
            pltpu.VMEM((1, CH), F32),
            pltpu.VMEM((3, 3, CH, CH), BF16),
            pltpu.VMEM((1, CH), F32),
            dma((12,)),
            pltpu.VMEM((TILES, RANKS, BLOCK, CH), BF16),
            pltpu.VMEM((TILES, RANKS, BLOCK, CH), BF16),
            pltpu.VMEM((TILES, SIDE + 2, WIDE, CH), F32),
            pltpu.VMEM((TILES, SIDE + 2, WIDE, CH), F32),
            pltpu.VMEM((12 * CH, 2 * CH), BF16),
            pltpu.VMEM((12 * CH, 2 * CH), BF16),
            pltpu.VMEM((TILES, 2, SIDE, 16, CH), F32),
            pltpu.VMEM((8 * SIDE, 9 * CH), BF16),
            pltpu.SMEM((8 * TILES,), jnp.int32),
            pltpu.VMEM((2, 3, WIDE, CH), F32),
            pltpu.VMEM((TILES, 4, WIDE, CH), F32),
            pltpu.VMEM((4, TILES * SIDE, 3 * CH), BF16),
            pltpu.VMEM((TILES, 2, SIDE, CH), F32),
            pltpu.VMEM((TILES, 2, SIDE // 16, 16, CH), F32),
            pltpu.VMEM((2, SIDE * 8, CH), F32),
            pltpu.VMEM((8, CH), jnp.int32),
            pltpu.VMEM((8, 8, CH), jnp.int32),
            pltpu.SMEM((8, 8, CH), jnp.int32),
            pltpu.VMEM((2, 32, SIDE, CH), BF16),
            pltpu.VMEM((2, 4, TILES, SIDE, CH), BF16),
            pltpu.VMEM((2, 4, TILES, SIDE, CH), BF16),
            pltpu.VMEM((2, 4, 16, CH), BF16),
            pltpu.VMEM((2, 4, 16, CH), BF16),
            dma((TILES,)),
            dma((TILES,)),
            dma((8,)),
            dma((8,)),
            dma,
            dma((2, 8)),
            dma((2, 8)),
            dma((2, 8)),
            dma((2, 8)),
        ],
        compiler_params=pltpu.CompilerParams(collective_id=0, has_side_effects=True, vmem_limit_bytes=48 << 20),
        name="level",
    )(
        *(
            pltpu.with_memory_space_constraint(v, pltpu.HBM)
            for v in (
                tile_order, table, latitude_rows, neighbours, rotations,
                w_first, b_first.reshape(1, CH), w_second, b_second.reshape(1, CH),
            )
        )
    )


def solution(mesh):
    return jax.shard_map(
        shards,
        mesh=mesh,
        in_specs=(
            P(None, ("face", "tile"), None),
            P(),
            P(("face", "tile"), None),
            P(("face", "tile"), None),
            P(),
            P(),
            P(),
            P(),
        ),
        out_specs=P(("face", "tile"), None, None, None),
        check_vma=False,
    )
```
